512 devices in a mesh: dp: 64 (over z, x_hi, core), mp: 8 (over x_lo, y).
Axes of the slice: x: 4 (x_hi: 2, x_lo: 2; x = x_hi * 2 + x_lo), y: 4, z: 16, core: 2. Of those that a mesh axis runs over, the one named last changes fastest.
Arguments:
- normed_input_rows: bfloat16 [24576, 8192], P('dp', 'mp'), may hold values from -6 to 6
- frozen_queries: bfloat16 [24576, 8192], P('dp', 'mp'), may hold values from -6 to 6
- frozen_keys: bfloat16 [24576, 1024], P('dp', 'mp'), may hold values from -6 to 6
- frozen_values: bfloat16 [24576, 1024], P('dp', 'mp'), may hold values from -6 to 6
- attention_output_gradient: bfloat16 [24576, 8192], P('dp', 'mp'), may hold values from -1.1953125 to 1.1953125
- adapter_down_weight: float32 [64, 8192, 192], P(None, ('mp', 'dp')), may hold values from -0.0625 to 0.0625
- adapter_up_query: float32 [64, 64, 8192], P(None, 'dp', 'mp'), may hold values from -0.75 to 0.75
- adapter_up_key_value: float32 [64, 64, 8, 256], P(None, 'dp', 'mp'), may hold values from -0.75 to 0.75
- document_numbers: int32 [24576], P('dp'), may hold values from 0 to 1535, as said below
- block_tenant_slot: int32 [192], P('dp'), may hold values from 0 to 1, as said below
- shard_tenant_table: int32 [64, 2], replicated, may hold values from 0 to 63, as said below
Outputs:
- grad_down: float32 [64, 8192, 192], P(None, ('mp', 'dp'))
- grad_upq: float32 [64, 64, 8192], P(None, 'dp', 'mp')
- grad_upkv: float32 [64, 64, 8, 256], P(None, 'dp', 'mp')
The draws below stay inside these ranges and needn't reach their ends.
Inputs may be any that keep to these rules, and one draw needn't show every extreme that they name: `document_numbers`: document numbers never fall along the rows; a document starts only at a multiple of 16 rows, always at the first row of each index of dp, at the last 16 rows of all, and wherever the slot of a block changes; a document's number is its first row divided by 16. `block_tenant_slot`: the 3 blocks of each index of dp name slots in an order that never falls, and every one of the 2 slots is named. `shard_tenant_table`: each row holds 2 distinct tenants.
All inputs are finite; a program needn't handle non-finite values.
Results may differ from the reference program's by a relative error of at most 0.012.
The reference program's roundings to bfloat16 on the way count: a program that leaves them out, or rounds other values in their place, can miss the bound.
Values sent between devices are 32-bit elements; how exact they have to be, the bound alone decides.
A program may use at most 64 MiB of HBM per device.

```python
import jax
import jax.numpy as jnp
from jax import lax

MODEL_WIDTH = 8192
QUERY_HEADS = 64
KEY_VALUE_HEADS = 8
HEAD_WIDTH = 128
ADAPTER_RANK = 64
TENANT_COUNT = 64
TENANT_BLOCK = 128
SLOTS = 2
TOKENS_PER_SHARD = 384
TOKEN_COUNT = 24576
N_DP = 64


def base_fields(key):
    query_noise = jax.random.normal(jax.random.fold_in(key, 11), (TOKEN_COUNT, QUERY_HEADS * HEAD_WIDTH), jnp.float32)
    key_perturbation = jax.random.normal(jax.random.fold_in(key, 12), (TOKEN_COUNT, KEY_VALUE_HEADS * HEAD_WIDTH), jnp.float32)
    query_noise = jnp.clip(query_noise, -6.0, 6.0)
    key_perturbation = jnp.clip(key_perturbation, -6.0, 6.0)
    return (query_noise, key_perturbation)


def draw_frozen_queries(key, part):
    return base_fields(key)[0].astype(jnp.bfloat16)


def draw_frozen_keys(key, part):
    return base_fields(key)[1].astype(jnp.bfloat16)


def tenant_layout(key):
    per_device = TOKENS_PER_SHARD // TENANT_BLOCK
    dev_keys = jax.random.split(jax.random.fold_in(key, 21), N_DP)
    order_ranks = jax.vmap(lambda single: jax.random.permutation(single, per_device - 1))(dev_keys)
    cut_flags = (order_ranks < SLOTS - 1).astype(jnp.int32)
    slot_rows = jnp.concatenate([jnp.zeros((N_DP, 1), jnp.int32), jnp.cumsum(cut_flags, axis=1).astype(jnp.int32)], axis=1)
    group_total = TOKENS_PER_SHARD // 16
    group_index = jnp.arange(group_total, dtype=jnp.int32)
    fresh_start = jax.random.randint(jax.random.fold_in(key, 22), (N_DP, group_total), 0, 4) == 0
    change = jnp.concatenate([jnp.zeros((N_DP, 1), bool), slot_rows[:, 1:] != slot_rows[:, :-1]], axis=1)
    at_block = group_index % (TENANT_BLOCK // 16) == 0
    change_groups = change[:, group_index // (TENANT_BLOCK // 16)] & at_block[None, :]
    start_flags = fresh_start | (group_index == 0)[None, :] | change_groups
    flat_flags = start_flags.reshape(-1)
    every_group = jnp.arange(N_DP * group_total, dtype=jnp.int32)
    flat_flags = flat_flags | (every_group == N_DP * group_total - 1)
    doc_groups = lax.cummax(jnp.where(flat_flags, every_group, 0).astype(jnp.int32), axis=0)
    return (slot_rows.reshape(-1), jnp.repeat(doc_groups, 16).astype(jnp.int32))


def draw_document_numbers(key, part):
    return tenant_layout(key)[1]


def draw_block_tenant_slot(key, part):
    return tenant_layout(key)[0]


def draw_shard_tenant_table(key, part):
    widest = (TENANT_COUNT - 1) // (SLOTS - 1)
    first_draw = jax.random.randint(jax.random.fold_in(key, 31), (N_DP,), 0, TENANT_COUNT)
    second_draw = jax.random.randint(jax.random.fold_in(key, 32), (N_DP,), 0, TENANT_COUNT)
    base_ids = jnp.minimum(first_draw, second_draw)
    stride = jax.random.randint(jax.random.fold_in(key, 33), (N_DP,), 1, widest + 1)
    row_index = jnp.arange(N_DP, dtype=jnp.int32)
    low_row = jax.random.randint(jax.random.fold_in(key, 34), (), 0, N_DP)
    high_row = (low_row + 1) % N_DP
    base_ids = jnp.where(row_index == low_row, 0, jnp.where(row_index == high_row, TENANT_COUNT - 1 - (SLOTS - 1) * widest, base_ids))
    stride = jnp.where((row_index == low_row) | (row_index == high_row), widest, stride)
    tenant_rows = (base_ids[:, None] + stride[:, None] * jnp.arange(SLOTS, dtype=jnp.int32)[None, :]) % TENANT_COUNT
    return tenant_rows.astype(jnp.int32)


def shard_levels(key, dims, cuts, least, top_value):
    level = 1.0
    for dim, blocks in cuts:
        steps = jax.random.uniform(jax.random.fold_in(jax.random.fold_in(key, 6), dim), (blocks,), jnp.float32, least / len(cuts), top_value / len(cuts))
        level = level * jnp.repeat(jnp.exp(steps), dims[dim] // blocks).reshape((-1,) + (1,) * (len(dims) - 1 - dim))
    return level


def scatter_about(own_key, shape, spread, limit, cuts=(), held_as=jnp.bfloat16):
    gain = shard_levels(own_key, shape, cuts, -0.22, 0.18) if cuts else 1.0
    result = jax.random.normal(own_key, shape, jnp.float32) * spread * gain
    return jnp.minimum(jnp.maximum(result, -limit), limit).astype(held_as)


def setup_inputs(seed: int = 0) -> dict:
    key_of = jax.random.split(jax.random.key(seed), 12)
    normed_input_rows = scatter_about(key_of[0], (TOKEN_COUNT, MODEL_WIDTH), 1.0, 6.0, ((0, 64), (1, 8)))
    frozen_queries = draw_frozen_queries(jax.random.fold_in(key_of[11], 71), 0)
    frozen_keys = draw_frozen_keys(jax.random.fold_in(key_of[11], 71), 0)
    frozen_values = scatter_about(key_of[3], (TOKEN_COUNT, KEY_VALUE_HEADS * HEAD_WIDTH), 1.0, 6.0, ((0, 64), (1, 8)))
    attention_output_gradient = scatter_about(key_of[4], (TOKEN_COUNT, QUERY_HEADS * HEAD_WIDTH), 0.2, 1.1953125, ((0, 64), (1, 8)))
    adapter_down_weight = scatter_about(key_of[5], (TENANT_COUNT, MODEL_WIDTH, 3 * ADAPTER_RANK), MODEL_WIDTH ** -0.5, 0.0625, ((1, 512),), jnp.float32)
    adapter_up_query = scatter_about(key_of[6], (TENANT_COUNT, ADAPTER_RANK, QUERY_HEADS * HEAD_WIDTH), ADAPTER_RANK ** -0.5, 0.75, ((1, 64), (2, 8)), jnp.float32)
    adapter_up_key_value = scatter_about(key_of[7], (TENANT_COUNT, ADAPTER_RANK, KEY_VALUE_HEADS, 2 * HEAD_WIDTH), ADAPTER_RANK ** -0.5, 0.75, ((1, 64), (2, 8)), jnp.float32)
    document_numbers = draw_document_numbers(jax.random.fold_in(key_of[11], 71), 0)
    block_tenant_slot = draw_block_tenant_slot(jax.random.fold_in(key_of[11], 71), 0)
    shard_tenant_table = draw_shard_tenant_table(jax.random.fold_in(key_of[11], 71), 0)
    return {"normed_input_rows": normed_input_rows, "frozen_queries": frozen_queries, "frozen_keys": frozen_keys, "frozen_values": frozen_values, "attention_output_gradient": attention_output_gradient, "adapter_down_weight": adapter_down_weight, "adapter_up_query": adapter_up_query, "adapter_up_key_value": adapter_up_key_value, "document_numbers": document_numbers, "block_tenant_slot": block_tenant_slot, "shard_tenant_table": shard_tenant_table}


ADAPTER_SCALE = 0.5
MASKED = -1e30
PRECISION_HIGH = lax.Precision.HIGHEST


def attention_grads(query_row_block, key_row_block, value_row_block, upstream, doc_row):
    row_total = query_row_block.shape[0]
    kv_heads = key_row_block.shape[1]
    groups = query_row_block.shape[1] // kv_heads
    head_size = query_row_block.shape[2]
    query_g = query_row_block.reshape(row_total, kv_heads, groups, head_size).astype(jnp.float32)
    key_f = key_row_block.astype(jnp.float32)
    value_f = value_row_block.astype(jnp.float32)
    upstream_g = upstream.reshape(row_total, kv_heads, groups, head_size).astype(jnp.float32)
    inverse = 1.0 / (head_size ** 0.5)
    scores = jnp.einsum("qkgd,jkd->kgqj", query_g, key_f, precision=PRECISION_HIGH) * inverse
    position = jnp.arange(row_total, dtype=jnp.int32)
    allowed = (doc_row[:, None] == doc_row[None, :]) & (position[:, None] >= position[None, :])
    scores = jnp.where(allowed, scores, MASKED)
    row_top = jnp.max(scores, axis=-1, keepdims=True)
    weights = jnp.exp(scores - row_top)
    attn_probs = weights / jnp.sum(weights, axis=-1, keepdims=True)
    probs_low = lax.optimization_barrier(attn_probs.astype(jnp.bfloat16)).astype(jnp.float32)
    grad_probs = jnp.einsum("qkgd,jkd->kgqj", upstream_g, value_f, precision=PRECISION_HIGH)
    row_inner = jnp.sum(attn_probs * grad_probs, axis=-1, keepdims=True)
    grad_scores = (attn_probs * (grad_probs - row_inner) * inverse).astype(jnp.bfloat16)
    grad_scores = lax.optimization_barrier(grad_scores).astype(jnp.float32)
    grad_query = jnp.einsum("kgqj,jkd->qkgd", grad_scores, key_f, precision=PRECISION_HIGH).reshape(row_total, -1)
    key_gradient = jnp.einsum("kgqj,qkgd->jkd", grad_scores, query_g, precision=PRECISION_HIGH).reshape(row_total, -1)
    value_gradient = jnp.einsum("kgqj,qkgd->jkd", probs_low, upstream_g, precision=PRECISION_HIGH).reshape(row_total, -1)
    return grad_query, key_gradient, value_gradient


def reference(normed_input_rows, frozen_queries, frozen_keys, frozen_values, attention_output_gradient, adapter_down_weight, adapter_up_query, adapter_up_key_value, document_numbers, block_tenant_slot, shard_tenant_table):
    total_blocks = TOKEN_COUNT // TENANT_BLOCK
    per_device = TOKENS_PER_SHARD // TENANT_BLOCK
    device_of = (jnp.arange(total_blocks, dtype=jnp.int32) // per_device).astype(jnp.int32)
    owner = shard_tenant_table[device_of, block_tenant_slot].astype(jnp.int32)
    row_blocks = normed_input_rows.reshape(total_blocks, TENANT_BLOCK, MODEL_WIDTH)

    def panels_of(tenant_index):
        query_adapter_panel = adapter_up_query[tenant_index]
        key_value_adapter_panel = adapter_up_key_value[tenant_index]
        key_adapter_panel = key_value_adapter_panel[:, :, :HEAD_WIDTH].reshape(ADAPTER_RANK, KEY_VALUE_HEADS * HEAD_WIDTH)
        value_adapter_panel = key_value_adapter_panel[:, :, HEAD_WIDTH:].reshape(ADAPTER_RANK, KEY_VALUE_HEADS * HEAD_WIDTH)
        return query_adapter_panel, key_adapter_panel, value_adapter_panel

    def forward_block(block_item):
        incoming_rows, tenant_index = block_item
        down_projected_rows = jnp.dot(incoming_rows.astype(jnp.float32), adapter_down_weight[tenant_index], precision=PRECISION_HIGH)
        query_adapter_panel, key_adapter_panel, value_adapter_panel = panels_of(tenant_index)
        query_addition = jnp.dot(down_projected_rows[:, :ADAPTER_RANK], query_adapter_panel, precision=PRECISION_HIGH)
        key_addition = jnp.dot(down_projected_rows[:, ADAPTER_RANK:2 * ADAPTER_RANK], key_adapter_panel, precision=PRECISION_HIGH)
        value_addition = jnp.dot(down_projected_rows[:, 2 * ADAPTER_RANK:], value_adapter_panel, precision=PRECISION_HIGH)
        return down_projected_rows, query_addition, key_addition, value_addition

    lowrank, query_addition, key_addition, value_addition = lax.map(forward_block, (row_blocks, owner))
    query_row_block = (frozen_queries.astype(jnp.float32) + ADAPTER_SCALE * query_addition.reshape(TOKEN_COUNT, QUERY_HEADS * HEAD_WIDTH)).astype(jnp.bfloat16)
    key_row_block = (frozen_keys.astype(jnp.float32) + ADAPTER_SCALE * key_addition.reshape(TOKEN_COUNT, KEY_VALUE_HEADS * HEAD_WIDTH)).astype(jnp.bfloat16)
    value_row_block = (frozen_values.astype(jnp.float32) + ADAPTER_SCALE * value_addition.reshape(TOKEN_COUNT, KEY_VALUE_HEADS * HEAD_WIDTH)).astype(jnp.bfloat16)

    def device_item(dev_item):
        q_dev, k_dev, v_dev, o_dev, doc_dev = dev_item
        return attention_grads(q_dev, k_dev, v_dev, o_dev, doc_dev)

    grad_query, key_gradient, value_gradient = lax.map(device_item, (
        query_row_block.reshape(N_DP, TOKENS_PER_SHARD, QUERY_HEADS, HEAD_WIDTH),
        key_row_block.reshape(N_DP, TOKENS_PER_SHARD, KEY_VALUE_HEADS, HEAD_WIDTH),
        value_row_block.reshape(N_DP, TOKENS_PER_SHARD, KEY_VALUE_HEADS, HEAD_WIDTH),
        attention_output_gradient.reshape(N_DP, TOKENS_PER_SHARD, QUERY_HEADS, HEAD_WIDTH),
        document_numbers.reshape(N_DP, TOKENS_PER_SHARD)))
    grad_query = grad_query.reshape(total_blocks, TENANT_BLOCK, QUERY_HEADS * HEAD_WIDTH)
    key_gradient = key_gradient.reshape(total_blocks, TENANT_BLOCK, KEY_VALUE_HEADS * HEAD_WIDTH)
    value_gradient = value_gradient.reshape(total_blocks, TENANT_BLOCK, KEY_VALUE_HEADS * HEAD_WIDTH)

    def backward_block(carry, block_item):
        acc_down, acc_q, acc_kv = carry
        incoming_rows, tenant_index, down_projected_rows, query_gradient_rows, key_gradient_rows, value_gradient_rows = block_item
        query_adapter_panel, key_adapter_panel, value_adapter_panel = panels_of(tenant_index)
        lowrank_gradient = ADAPTER_SCALE * jnp.concatenate([
            jnp.dot(query_gradient_rows, query_adapter_panel.T, precision=PRECISION_HIGH),
            jnp.dot(key_gradient_rows, key_adapter_panel.T, precision=PRECISION_HIGH),
            jnp.dot(value_gradient_rows, value_adapter_panel.T, precision=PRECISION_HIGH)], axis=-1)
        term_down = jnp.dot(incoming_rows.astype(jnp.float32).T, lowrank_gradient, precision=PRECISION_HIGH)
        query_term = ADAPTER_SCALE * jnp.dot(down_projected_rows[:, :ADAPTER_RANK].T, query_gradient_rows, precision=PRECISION_HIGH)
        key_term = (ADAPTER_SCALE * jnp.dot(down_projected_rows[:, ADAPTER_RANK:2 * ADAPTER_RANK].T, key_gradient_rows, precision=PRECISION_HIGH)).reshape(ADAPTER_RANK, KEY_VALUE_HEADS, HEAD_WIDTH)
        value_term = (ADAPTER_SCALE * jnp.dot(down_projected_rows[:, 2 * ADAPTER_RANK:].T, value_gradient_rows, precision=PRECISION_HIGH)).reshape(ADAPTER_RANK, KEY_VALUE_HEADS, HEAD_WIDTH)
        term_kv = jnp.concatenate([key_term, value_term], axis=-1)
        return (acc_down.at[tenant_index].add(term_down), acc_q.at[tenant_index].add(query_term), acc_kv.at[tenant_index].add(term_kv)), None

    start = (jnp.zeros((TENANT_COUNT, MODEL_WIDTH, 3 * ADAPTER_RANK), jnp.float32),
             jnp.zeros((TENANT_COUNT, ADAPTER_RANK, QUERY_HEADS * HEAD_WIDTH), jnp.float32),
             jnp.zeros((TENANT_COUNT, ADAPTER_RANK, KEY_VALUE_HEADS, 2 * HEAD_WIDTH), jnp.float32))
    (grad_down, grad_upq, grad_upkv), _ = lax.scan(backward_block, start, (row_blocks, owner, lowrank, grad_query, key_gradient, value_gradient))
    return grad_down, grad_upq, grad_upkv
```

```python
import functools

import jax
import jax.numpy as jnp
from jax import lax
from jax.experimental import pallas as pl
from jax.experimental.pallas import tpu as pltpu
from jax.sharding import PartitionSpec as P

ADAPTER_SCALE = 0.5
MASKED = -1e30
MESH = pl.DeviceIdType.MESH
LANES = 128
F32 = jnp.float32
BF16 = jnp.bfloat16


def dot(a, b, ca, cb):
    return lax.dot_general(a, b, (((ca,), (cb,)), ((), ())), preferred_element_type=F32)


def parts(a):
    high = a.astype(BF16)
    return high, (a - high.astype(F32)).astype(BF16)


def dot_exact_left(a, b, ca, cb):
    high, low = parts(b)
    return dot(a, high, ca, cb) + dot(a, low, ca, cb)


def dot_both(a, b, ca, cb):
    a_high, a_low = parts(a)
    b_high, b_low = parts(b)
    return dot(a_high, b_high, ca, cb) + (dot(a_high, b_low, ca, cb) + dot(a_low, b_high, ca, cb))


def barrier(dp, mp, n_dp, n_mp):
    sem = pltpu.get_barrier_semaphore()

    @pl.loop(1, n_dp)
    def _(k):
        pl.semaphore_signal(
            sem, inc=1, device_id={"dp": lax.rem(dp + k, n_dp)}, device_id_type=MESH
        )

    for k in range(1, n_mp):
        pl.semaphore_signal(
            sem, inc=1, device_id={"mp": lax.rem(mp + k, n_mp)}, device_id_type=MESH
        )
    return lambda: pl.semaphore_wait(sem, n_dp - 1 + n_mp - 1)


class Exchange:
    def __init__(self, source, target, send, recv, dp, n_dp):
        self.source, self.target, self.send, self.recv = source, target, send, recv
        self.dp, self.n_dp = dp, n_dp

    def piece(self, k, peer, slot):
        return pltpu.make_async_remote_copy(
            src_ref=self.source.at[peer],
            dst_ref=self.target.at[slot],
            send_sem=self.send.at[k],
            recv_sem=self.recv.at[k],
            device_id={"dp": peer},
            device_id_type=MESH,
        )

    def start(self, k):
        self.piece(k, lax.rem(self.dp + k, self.n_dp), self.dp).start()

    def keep(self):
        self.target[pl.ds(self.dp, 1)] = self.source[pl.ds(self.dp, 1)]

    def wait_recv(self):
        @pl.loop(1, self.n_dp)
        def _(k):
            origin = lax.rem(self.dp + self.n_dp - k, self.n_dp)
            self.piece(k, origin, origin).wait_recv()

    def wait_send(self):
        @pl.loop(1, self.n_dp)
        def _(k):
            self.piece(k, lax.rem(self.dp + k, self.n_dp), self.dp).wait_send()


def start_all(exchanges, n_dp):
    for group in exchanges:

        @pl.loop(0, n_dp - 1)
        def _(i):
            half = lax.div(i + 2, 2)
            k = jnp.where(lax.rem(i, 2) == 0, half, n_dp - half)
            for exchange in group:
                exchange.start(k)


class SumOverMp:
    def __init__(self, partial, landed, total, sems, mp, n_mp):
        self.partial, self.landed, self.total = partial, landed, total
        self.mp, self.n_mp = mp, n_mp
        self.rows = partial.shape[0] // n_mp
        self.sems = sems

    def rows_of(self, p):
        return pl.ds(pl.multiple_of(p * self.rows, 8), self.rows)

    def copy(self, k, second):
        peer = lax.rem(self.mp + k, self.n_mp)
        if second:
            source = target = self.total.at[self.rows_of(self.mp)]
        else:
            source, target = self.partial.at[self.rows_of(peer)], self.landed.at[k]
        return pltpu.make_async_remote_copy(
            src_ref=source,
            dst_ref=target,
            send_sem=self.sems.at[2 * second, k],
            recv_sem=self.sems.at[2 * second + 1, k],
            device_id={"mp": peer},
            device_id_type=MESH,
        )

    def landed_total(self, k):
        origin = lax.rem(self.mp + self.n_mp - k, self.n_mp)
        return pltpu.make_async_remote_copy(
            src_ref=self.total.at[self.rows_of(origin)],
            dst_ref=self.total.at[self.rows_of(origin)],
            send_sem=self.sems.at[2, k],
            recv_sem=self.sems.at[3, k],
            device_id={"mp": origin},
            device_id_type=MESH,
        )

    def run(self):
        for k in range(1, self.n_mp):
            self.copy(k, 0).start()
        mine = self.partial[self.rows_of(self.mp)]
        for k in range(1, self.n_mp):
            self.copy(k, 0).wait_recv()
            mine = mine + self.landed[k]
        self.total[self.rows_of(self.mp)] = mine
        for k in range(1, self.n_mp):
            self.copy(k, 1).start()
        for k in range(1, self.n_mp):
            self.landed_total(k).wait_recv()

    def finish(self):
        for k in range(1, self.n_mp):
            self.copy(k, 0).wait_send()
            self.copy(k, 1).wait_send()


def store_packed(ref, wide, narrow):
    rows = wide.shape[0]
    half = rows // 2
    ref[0:rows] = wide
    ref[rows : rows + half] = jnp.concatenate([narrow[0:half], narrow[half:rows]], axis=1)


def load_packed(ref, rows):
    half = rows // 2
    tail = ref[rows : rows + half]
    width = tail.shape[1] // 2
    return ref[0:rows], jnp.concatenate([tail[:, :width], tail[:, width:]], axis=0)


def whole_kernel(
    n_dp,
    n_mp,
    rows_ref,
    queries_ref,
    keys_ref,
    values_ref,
    upstream_ref,
    down_ref,
    upq_ref,
    upkv_ref,
    slot_ref,
    doc_col_ref,
    doc_row_ref,
    table_ref,
    got_down_ref,
    got_upq_ref,
    got_upkv_ref,
    send_down,
    send_upq,
    send_upkv,
    recv_down,
    recv_upq,
    recv_upkv,
    partial,
    landed,
    total,
    partial_back,
    landed_back,
    total_back,
    bias,
    send_upq_back,
    send_upkv_back,
    send_down_back,
    exchange_sems,
    sum_sems,
):
    dp, mp = lax.axis_index("dp"), lax.axis_index("mp")
    row_total = rows_ref.shape[0]
    rank = down_ref.shape[2] // 3
    wide = 2 * rank
    columns = down_ref.shape[1]
    heads = queries_ref.shape[1] // LANES
    inverse = 1.0 / float(LANES) ** 0.5

    arrived = barrier(dp, mp, n_dp, n_mp)

    @pl.loop(0, n_dp)
    def _(d):
        first, second = table_ref[d, 0], table_ref[d, 1]
        a, b = down_ref[first], down_ref[second]
        send_down[d] = jnp.concatenate(
            [a[:, :wide], b[:, :wide], jnp.concatenate([a[:, wide:], b[:, wide:]], axis=1)],
            axis=0,
        )
        send_upq[d] = jnp.concatenate([upq_ref[first], upq_ref[second]], axis=0)
        send_upkv[d, 0:2] = upkv_ref[first]
        send_upkv[d, 2:4] = upkv_ref[second]

    arrived()

    def exchange(index, source, target):
        return Exchange(
            source, target, exchange_sems.at[2 * index], exchange_sems.at[2 * index + 1], dp, n_dp
        )

    down_in = exchange(0, send_down, recv_down)
    upkv_in = exchange(1, send_upkv, recv_upkv)
    upq_in = exchange(2, send_upq, recv_upq)
    start_all([[down_in], [upkv_in, upq_in]], n_dp)
    down_in.keep()
    upkv_in.keep()
    upq_in.keep()

    position_key = lax.broadcasted_iota(jnp.int32, (row_total, row_total), 0)
    position_query = lax.broadcasted_iota(jnp.int32, (row_total, row_total), 1)
    joined = (doc_col_ref[...] == doc_row_ref[...]) & (position_key <= position_query)
    bias[...] = jnp.where(joined, 0.0, MASKED).astype(F32)

    in_second = slot_ref[...]
    in_first = 1.0 - in_second

    down_in.wait_recv()
    rows = rows_ref[...]

    def panel(i):
        return recv_down[:, i * columns : (i + 1) * columns, :].reshape(n_dp * columns, LANES)

    low_wide = (
        dot_exact_left(rows, panel(0), 1, 0) * in_first
        + dot_exact_left(rows, panel(1), 1, 0) * in_second
    )
    both = dot_exact_left(rows, panel(2), 1, 0)
    low_narrow = both[:, :rank] * in_first[:, :rank] + both[:, rank:] * in_second[:, :rank]
    store_packed(partial, low_wide, low_narrow)
    low_sum = SumOverMp(partial, landed, total, sum_sems.at[0], mp, n_mp)
    low_sum.run()
    low_wide, low_v = load_packed(total, row_total)

    def by_slot(low):
        return jnp.concatenate(
            [low * in_first[:, :rank], low * in_second[:, :rank]], axis=1
        )

    low_q = by_slot(low_wide[:, :rank])
    low_k = by_slot(low_wide[:, rank:])
    low_v = by_slot(low_v)

    upkv_in.wait_recv()
    upq_in.wait_recv()

    up_k = jnp.concatenate([recv_upkv[:, 0, :], recv_upkv[:, 2, :]], axis=0)
    up_v = jnp.concatenate([recv_upkv[:, 1, :], recv_upkv[:, 3, :]], axis=0)

    def adapted(frozen, low, panel):
        return (frozen.astype(F32) + ADAPTER_SCALE * dot_both(low, panel, 1, 0)).astype(BF16)

    key = adapted(keys_ref[...], low_k, up_k)
    value = adapted(values_ref[...], low_v, up_v)
    low_q_parts = parts(low_q)

    def dot_low_q(grad):
        high, low = parts(grad)
        a_high, a_low = low_q_parts
        return dot(a_high, high, 0, 0) + (dot(a_high, low, 0, 0) + dot(a_low, high, 0, 0))

    grad_key = jnp.zeros((row_total, LANES), F32)
    grad_value = jnp.zeros((row_total, LANES), F32)
    grad_low_q = jnp.zeros((row_total, wide), F32)
    for head in range(heads):
        lanes = slice(head * LANES, (head + 1) * LANES)
        panel_q = jnp.concatenate(
            [recv_upq[:, head, :], recv_upq[:, heads + head, :]], axis=0
        )
        query = adapted(queries_ref[:, lanes], low_q, panel_q)
        upstream = upstream_ref[:, lanes]
        scores = dot(key, query, 1, 1) * inverse + bias[...]
        weights = jnp.exp(scores - jnp.max(scores, axis=0, keepdims=True))
        probs = weights / jnp.sum(weights, axis=0, keepdims=True)
        grad_probs = dot(value, upstream, 1, 1)
        inner = jnp.sum(probs * grad_probs, axis=0, keepdims=True)
        grad_scores = (probs * (grad_probs - inner) * inverse).astype(BF16)
        grad_key = grad_key + dot(grad_scores, query, 1, 0)
        grad_value = grad_value + dot(probs.astype(BF16), upstream, 1, 0)
        grad_head = dot(grad_scores, key, 0, 0)
        grad_low_q = grad_low_q + dot_both(grad_head, panel_q, 1, 1)
        term = ADAPTER_SCALE * dot_low_q(grad_head)
        send_upq_back[:, head, :] = term[:rank]
        send_upq_back[:, heads + head, :] = term[rank:]
    term = ADAPTER_SCALE * dot_both(low_k, grad_key, 0, 0)
    send_upkv_back[:, 0, :] = term[:rank]
    send_upkv_back[:, 2, :] = term[rank:]
    term = ADAPTER_SCALE * dot_both(low_v, grad_value, 0, 0)
    send_upkv_back[:, 1, :] = term[:rank]
    send_upkv_back[:, 3, :] = term[rank:]

    upkv_back = exchange(3, send_upkv_back, got_upkv_ref)
    upq_back = exchange(4, send_upq_back, got_upq_ref)
    down_back = exchange(5, send_down_back, got_down_ref)

    def of_slot(grad):
        return ADAPTER_SCALE * (
            grad[:, :rank] * in_first[:, :rank] + grad[:, rank:] * in_second[:, :rank]
        )

    grad_low_k = dot_both(grad_key, up_k, 1, 1)
    grad_low_v = dot_both(grad_value, up_v, 1, 1)
    store_packed(
        partial_back,
        jnp.concatenate([of_slot(grad_low_q), of_slot(grad_low_k)], axis=1),
        of_slot(grad_low_v),
    )
    start_all([[upkv_back, upq_back]], n_dp)
    upkv_back.keep()
    upq_back.keep()
    grad_sum = SumOverMp(partial_back, landed_back, total_back, sum_sems.at[1], mp, n_mp)
    grad_sum.run()
    grad_wide, grad_narrow = load_packed(total_back, row_total)

    def down_term(i, grad):
        send_down_back[:, i * columns : (i + 1) * columns, :] = dot_exact_left(
            rows, grad, 0, 0
        ).reshape(n_dp, columns, LANES)

    down_term(0, grad_wide * in_first)
    down_term(1, grad_wide * in_second)
    down_term(
        2,
        jnp.concatenate(
            [grad_narrow * in_first[:, :rank], grad_narrow * in_second[:, :rank]], axis=1
        ),
    )
    start_all([[down_back]], n_dp)
    down_back.keep()

    down_in.wait_send()
    upkv_in.wait_send()
    upq_in.wait_send()
    low_sum.finish()
    grad_sum.finish()
    for one in (upkv_back, upq_back, down_back):
        one.wait_recv()
        one.wait_send()


def owner_kernel(down_ref, upq_ref, upkv_ref, table_ref, out_down, out_upq, out_upkv):
    rank = out_down.shape[2] // 3
    wide = 2 * rank
    columns = out_down.shape[1]
    heads = out_upq.shape[1]
    out_down[...] = jnp.zeros_like(out_down)
    out_upq[...] = jnp.zeros_like(out_upq)
    out_upkv[...] = jnp.zeros_like(out_upkv)

    @pl.loop(0, down_ref.shape[0])
    def _(j):
        both = down_ref[j, 2 * columns : 3 * columns]
        for slot in range(2):
            tenant = table_ref[j, slot]
            out_down[tenant] += jnp.concatenate(
                [
                    down_ref[j, slot * columns : (slot + 1) * columns],
                    both[:, slot * rank : (slot + 1) * rank],
                ],
                axis=1,
            )
            out_upq[tenant] += upq_ref[j, slot * heads : (slot + 1) * heads]
            out_upkv[tenant] += upkv_ref[j, slot * 2 : (slot + 1) * 2]


def on_device(
    normed_input_rows,
    frozen_queries,
    frozen_keys,
    frozen_values,
    attention_output_gradient,
    adapter_down_weight,
    adapter_up_query,
    adapter_up_key_value,
    document_numbers,
    block_tenant_slot,
    shard_tenant_table,
    *,
    n_dp,
    n_mp,
):
    row_total = normed_input_rows.shape[0]
    tenants, columns, three_rank = adapter_down_weight.shape
    heads = frozen_queries.shape[1] // LANES
    upq = adapter_up_query.reshape(tenants, heads, LANES)
    upkv = adapter_up_key_value.reshape(tenants, 2, LANES)
    slots = jnp.broadcast_to(
        jnp.repeat(block_tenant_slot.astype(F32), row_total // block_tenant_slot.shape[0])[:, None],
        (row_total, LANES),
    )
    down_shape = (n_dp, 3 * columns, LANES)
    upq_shape = (n_dp, 2 * heads, LANES)
    upkv_shape = (n_dp, 4, LANES)
    packed = row_total * three_rank // LANES
    vmem = pl.BlockSpec(memory_space=pltpu.VMEM)
    smem = pl.BlockSpec(memory_space=pltpu.SMEM)
    sums = [
        pltpu.VMEM((packed, LANES), F32),
        pltpu.VMEM((n_mp, packed // n_mp, LANES), F32),
        pltpu.VMEM((packed, LANES), F32),
    ]
    got = pl.pallas_call(
        functools.partial(whole_kernel, n_dp, n_mp),
        out_shape=[jax.ShapeDtypeStruct(s, F32) for s in (down_shape, upq_shape, upkv_shape)],
        in_specs=[vmem] * 11 + [smem],
        out_specs=[vmem] * 3,
        scratch_shapes=[
            pltpu.VMEM(down_shape, F32),
            pltpu.VMEM(upq_shape, F32),
            pltpu.VMEM(upkv_shape, F32),
            pltpu.VMEM(down_shape, F32),
            pltpu.VMEM(upq_shape, F32),
            pltpu.VMEM(upkv_shape, F32),
            *sums,
            *sums,
            pltpu.VMEM((row_total, row_total), F32),
            pltpu.VMEM(upq_shape, F32),
            pltpu.VMEM(upkv_shape, F32),
            pltpu.VMEM(down_shape, F32),
            pltpu.SemaphoreType.DMA((12, n_dp)),
            pltpu.SemaphoreType.DMA((2, 4, n_mp)),
        ],
        compiler_params=pltpu.CompilerParams(
            collective_id=0, has_side_effects=True, vmem_limit_bytes=60 * 1024 * 1024
        ),
        name="whole",
    )(
        normed_input_rows,
        frozen_queries,
        frozen_keys,
        frozen_values,
        attention_output_gradient,
        adapter_down_weight,
        upq,
        upkv,
        slots,
        document_numbers[:, None],
        document_numbers[None, :],
        shard_tenant_table,
    )
    grad_down, grad_upq, grad_upkv = pl.pallas_call(
        owner_kernel,
        out_shape=[
            jax.ShapeDtypeStruct(adapter_down_weight.shape, F32),
            jax.ShapeDtypeStruct(upq.shape, F32),
            jax.ShapeDtypeStruct(upkv.shape, F32),
        ],
        in_specs=[vmem] * 3 + [smem],
        out_specs=[vmem] * 3,
        name="owner",
    )(*got, shard_tenant_table)
    return (
        grad_down,
        grad_upq.reshape(adapter_up_query.shape),
        grad_upkv.reshape(adapter_up_key_value.shape),
    )


def solution(mesh):
    placed = (
        P("dp", "mp"),
        P("dp", "mp"),
        P("dp", "mp"),
        P("dp", "mp"),
        P("dp", "mp"),
        P(None, ("mp", "dp"), None),
        P(None, "dp", "mp"),
        P(None, "dp", "mp", None),
        P("dp"),
        P("dp"),
        P(),
    )
    return jax.shard_map(
        functools.partial(on_device, n_dp=mesh.shape["dp"], n_mp=mesh.shape["mp"]),
        mesh=mesh,
        in_specs=placed,
        out_specs=(P(None, ("mp", "dp"), None), P(None, "dp", "mp"), P(None, "dp", "mp", None)),
        check_vma=False,
    )
```

```python
import functools

import jax
import jax.numpy as jnp
from jax import lax
from jax.experimental import pallas as pl
from jax.experimental.pallas import tpu as pltpu
from jax.sharding import PartitionSpec as P

ADAPTER_SCALE = 0.5
MASKED = -1e30
MESH = pl.DeviceIdType.MESH
LANES = 128
DOC_ROWS = 16
F32 = jnp.float32
BF16 = jnp.bfloat16


def dot(a, b, ca, cb):
    return lax.dot_general(a, b, (((ca,), (cb,)), ((), ())), preferred_element_type=F32)


def parts(a):
    high = a.astype(BF16)
    return high, (a - high.astype(F32)).astype(BF16)


def dot_exact_left(a, b, ca, cb):
    high, low = parts(b)
    return dot(a, high, ca, cb) + dot(a, low, ca, cb)


def dot_both(a, b, ca, cb):
    a_high, a_low = parts(a)
    b_high, b_low = parts(b)
    return dot(a_high, b_high, ca, cb) + (dot(a_high, b_low, ca, cb) + dot(a_low, b_high, ca, cb))


def barrier(dp, mp, n_dp, n_mp):
    sem = pltpu.get_barrier_semaphore()

    @pl.loop(1, n_dp)
    def _(k):
        pl.semaphore_signal(
            sem, inc=1, device_id={"dp": lax.rem(dp + k, n_dp)}, device_id_type=MESH
        )

    for k in range(1, n_mp):
        pl.semaphore_signal(
            sem, inc=1, device_id={"mp": lax.rem(mp + k, n_mp)}, device_id_type=MESH
        )
    return lambda: pl.semaphore_wait(sem, n_dp - 1 + n_mp - 1)


class Exchange:
    def __init__(self, source, target, send, recv, dp, n_dp):
        self.source, self.target, self.send, self.recv = source, target, send, recv
        self.dp, self.n_dp = dp, n_dp

    def piece(self, k, peer, slot):
        return pltpu.make_async_remote_copy(
            src_ref=self.source.at[peer],
            dst_ref=self.target.at[slot],
            send_sem=self.send.at[k],
            recv_sem=self.recv.at[k],
            device_id={"dp": peer},
            device_id_type=MESH,
        )

    def start(self, k):
        self.piece(k, lax.rem(self.dp + k, self.n_dp), self.dp).start()

    def keep(self):
        self.target[pl.ds(self.dp, 1)] = self.source[pl.ds(self.dp, 1)]

    def wait_recv(self):
        @pl.loop(1, self.n_dp)
        def _(k):
            origin = lax.rem(self.dp + self.n_dp - k, self.n_dp)
            self.piece(k, origin, origin).wait_recv()

    def wait_send(self):
        @pl.loop(1, self.n_dp)
        def _(k):
            self.piece(k, lax.rem(self.dp + k, self.n_dp), self.dp).wait_send()


def start_all(exchanges, n_dp):
    for group in exchanges:

        @pl.loop(0, n_dp - 1)
        def _(i):
            half = lax.div(i + 2, 2)
            k = jnp.where(lax.rem(i, 2) == 0, half, n_dp - half)
            for exchange in group:
                exchange.start(k)


class SumOverMp:
    def __init__(self, partial, landed, total, sems, mp, n_mp):
        self.partial, self.landed, self.total = partial, landed, total
        self.mp, self.n_mp = mp, n_mp
        self.rows = partial.shape[0] // n_mp
        self.sems = sems

    def rows_of(self, p):
        return pl.ds(pl.multiple_of(p * self.rows, 8), self.rows)

    def copy(self, k, second):
        peer = lax.rem(self.mp + k, self.n_mp)
        if second:
            source = target = self.total.at[self.rows_of(self.mp)]
        else:
            source, target = self.partial.at[self.rows_of(peer)], self.landed.at[k]
        return pltpu.make_async_remote_copy(
            src_ref=source,
            dst_ref=target,
            send_sem=self.sems.at[2 * second, k],
            recv_sem=self.sems.at[2 * second + 1, k],
            device_id={"mp": peer},
            device_id_type=MESH,
        )

    def landed_total(self, k):
        origin = lax.rem(self.mp + self.n_mp - k, self.n_mp)
        return pltpu.make_async_remote_copy(
            src_ref=self.total.at[self.rows_of(origin)],
            dst_ref=self.total.at[self.rows_of(origin)],
            send_sem=self.sems.at[2, k],
            recv_sem=self.sems.at[3, k],
            device_id={"mp": origin},
            device_id_type=MESH,
        )

    def scatter(self):
        for k in range(1, self.n_mp):
            self.copy(k, 0).start()

    def gather(self):
        mine = self.partial[self.rows_of(self.mp)]
        for k in range(1, self.n_mp):
            self.copy(k, 0).wait_recv()
            mine = mine + self.landed[k]
        self.total[self.rows_of(self.mp)] = mine
        for k in range(1, self.n_mp):
            self.copy(k, 1).start()

    def arrive(self):
        for k in range(1, self.n_mp):
            self.landed_total(k).wait_recv()

    def finish(self):
        for k in range(1, self.n_mp):
            self.copy(k, 0).wait_send()
            self.copy(k, 1).wait_send()


def store_packed(ref, wide, narrow):
    rows = wide.shape[0]
    half = rows // 2
    ref[0:rows] = wide
    ref[rows : rows + half] = jnp.concatenate([narrow[0:half], narrow[half:rows]], axis=1)


def load_packed(ref, rows):
    half = rows // 2
    tail = ref[rows : rows + half]
    width = tail.shape[1] // 2
    return ref[0:rows], jnp.concatenate([tail[:, :width], tail[:, width:]], axis=0)


def whole_kernel(
    n_dp,
    n_mp,
    groups,
    rows_hbm,
    queries_hbm,
    keys_hbm,
    values_hbm,
    upstream_hbm,
    down_hbm,
    upq_hbm,
    upkv_hbm,
    slot_ref,
    doc_ref,
    table_ref,
    got_down_ref,
    got_upq_ref,
    got_upkv_ref,
    rows_ref,
    queries_ref,
    keys_ref,
    values_ref,
    upstream_ref,
    down_ref,
    upq_ref,
    upkv_ref,
    send_down,
    send_upq,
    send_upkv,
    recv_down,
    recv_upq,
    recv_upkv,
    partial,
    landed,
    total,
    partial_back,
    landed_back,
    total_back,
    rows_turned,
    bias,
    grad_query_turned,
    grad_key,
    grad_value,
    send_upq_back,
    send_upkv_back,
    send_down_back,
    load_sems,
    exchange_sems,
    sum_sems,
):
    dp, mp = lax.axis_index("dp"), lax.axis_index("mp")
    row_total = rows_ref.shape[0]
    rank = down_ref.shape[2] // 3
    wide = 2 * rank
    columns = down_ref.shape[1]
    heads = queries_ref.shape[1] // LANES
    per_group = heads // groups
    group_lanes = per_group * LANES
    blocks = slot_ref.shape[0]
    block_rows = row_total // blocks
    inverse = 1.0 / float(LANES) ** 0.5

    loads = [
        pltpu.make_async_copy(source, target, load_sems.at[i])
        for i, (source, target) in enumerate(
            [
                (down_hbm, down_ref),
                (upq_hbm, upq_ref),
                (upkv_hbm, upkv_ref),
                (rows_hbm, rows_ref),
                (keys_hbm, keys_ref),
                (values_hbm, values_ref),
                (queries_hbm, queries_ref),
                (upstream_hbm, upstream_ref),
            ]
        )
    ]
    for load in loads:
        load.start()
    arrived = barrier(dp, mp, n_dp, n_mp)
    for load in loads[:3]:
        load.wait()

    @pl.loop(0, n_dp)
    def _(d):
        first, second = table_ref[0, d], table_ref[1, d]
        a, b = down_ref[first], down_ref[second]
        send_down[d] = jnp.concatenate(
            [a[:, :wide], b[:, :wide], jnp.concatenate([a[:, wide:], b[:, wide:]], axis=1)],
            axis=0,
        )
        a, b = upq_ref[first], upq_ref[second]
        for g in range(groups):
            span = slice(g * per_group, (g + 1) * per_group)
            send_upq[g, d] = jnp.concatenate([a[span], b[span]], axis=0)
        send_upkv[d, 0:2] = upkv_ref[first]
        send_upkv[d, 2:4] = upkv_ref[second]

    arrived()

    def exchange(index, source, target):
        return Exchange(
            source, target, exchange_sems.at[2 * index], exchange_sems.at[2 * index + 1], dp, n_dp
        )

    down_in = exchange(0, send_down, recv_down)
    upkv_in = exchange(1, send_upkv, recv_upkv)
    upq_in = [exchange(2 + g, send_upq.at[g], recv_upq.at[g]) for g in range(groups)]
    upkv_back = exchange(2 + groups, send_upkv_back, got_upkv_ref)
    down_back = exchange(3 + groups, send_down_back, got_down_ref)
    upq_back = [
        exchange(4 + groups + g, send_upq_back.at[g], got_upq_ref.at[g]) for g in range(groups)
    ]
    start_all([[down_in], [upkv_in, upq_in[0]]] + [[one] for one in upq_in[1:]], n_dp)
    for one in [down_in, upkv_in] + upq_in:
        one.keep()

    lane = lax.broadcasted_iota(jnp.int32, (1, row_total), 1)
    doc_lane = jnp.zeros((1, row_total), jnp.int32)
    for start in range(0, row_total, DOC_ROWS):
        doc_lane = jnp.where(lane >= start, doc_ref[start], doc_lane)
    sub = lax.broadcasted_iota(jnp.int32, (DOC_ROWS, row_total), 0)
    for start in range(0, row_total, DOC_ROWS):
        joined = (doc_lane == doc_ref[start]) & (sub + start <= lane)
        bias[start : start + DOC_ROWS] = jnp.where(joined, 0.0, MASKED).astype(F32)
    in_second = jnp.concatenate(
        [jnp.full((block_rows, LANES), slot_ref[b].astype(F32)) for b in range(blocks)], axis=0
    )
    in_first = 1.0 - in_second
    for load in loads[3:]:
        load.wait()
    rows = rows_ref[...]
    rows_turned[...] = rows.T

    down_in.wait_recv()
    panels = jnp.concatenate(
        [
            recv_down[:, i * columns : (i + 1) * columns, :].reshape(n_dp * columns, LANES)
            for i in range(3)
        ],
        axis=1,
    )
    low = dot(rows, jnp.concatenate(parts(panels), axis=1), 1, 0)
    low = low[:, : 3 * LANES] + low[:, 3 * LANES :]
    low_wide = low[:, :LANES] * in_first + low[:, LANES : 2 * LANES] * in_second
    both = low[:, 2 * LANES :]
    low_narrow = both[:, :rank] * in_first[:, :rank] + both[:, rank:] * in_second[:, :rank]
    store_packed(partial, low_wide, low_narrow)
    low_sum = SumOverMp(partial, landed, total, sum_sems.at[0], mp, n_mp)
    low_sum.scatter()
    low_sum.gather()
    low_sum.arrive()
    low_wide, low_v = load_packed(total, row_total)

    def by_slot(low):
        return jnp.concatenate(
            [low * in_first[:, :rank], low * in_second[:, :rank]], axis=1
        )

    low_q = by_slot(low_wide[:, :rank])
    low_k = by_slot(low_wide[:, rank:])
    low_v = by_slot(low_v)

    def adapted(frozen, low, panel):
        return (frozen.astype(F32) + ADAPTER_SCALE * dot_both(low, panel, 1, 0)).astype(BF16)

    upkv_in.wait_recv()
    up_k = jnp.concatenate([recv_upkv[:, 0, :], recv_upkv[:, 2, :]], axis=0)
    up_v = jnp.concatenate([recv_upkv[:, 1, :], recv_upkv[:, 3, :]], axis=0)
    key = adapted(keys_ref[...], low_k, up_k)
    value = adapted(values_ref[...], low_v, up_v)
    key_turned = key.T
    grad_key[...] = jnp.zeros_like(grad_key)
    grad_value[...] = jnp.zeros_like(grad_value)
    grad_low_q = jnp.zeros((wide, row_total), F32)
    for g in range(groups):
        lanes = slice(g * group_lanes, (g + 1) * group_lanes)
        upq_in[g].wait_recv()
        panel = jnp.concatenate(
            [
                jnp.concatenate(
                    [recv_upq[g, :, h, :], recv_upq[g, :, per_group + h, :]], axis=0
                )
                for h in range(per_group)
            ],
            axis=1,
        )
        query = adapted(queries_ref[:, lanes], low_q, panel)
        upstream = upstream_ref[:, lanes]

        def stacked(a, first):
            return jnp.concatenate(
                [
                    a[first : first + block_rows, h * LANES : (h + 1) * LANES]
                    for h in range(per_group)
                ],
                axis=0,
            )

        for b in range(blocks):
            first, last = b * block_rows, (b + 1) * block_rows
            query_b, upstream_b = stacked(query, first), stacked(upstream, first)
            mask = jnp.concatenate([bias[0:last, first:last]] * per_group, axis=1)
            scores = dot(key[:last], query_b, 1, 1) * inverse + mask
            weights = jnp.exp(scores - jnp.max(scores, axis=0, keepdims=True))
            probs = weights * (1.0 / jnp.sum(weights, axis=0, keepdims=True))
            grad_probs = dot(value[:last], upstream_b, 1, 1)
            inner = jnp.sum(probs * grad_probs, axis=0, keepdims=True)
            grad_scores = (probs * (grad_probs - inner) * inverse).astype(BF16)
            grad_key[0:last] += dot(grad_scores, query_b, 1, 0)
            grad_value[0:last] += dot(probs.astype(BF16), upstream_b, 1, 0)
            turned = dot(key_turned[:, :last], grad_scores, 1, 0)
            for h in range(per_group):
                grad_query_turned[h * LANES : (h + 1) * LANES, first:last] = turned[
                    :, h * block_rows : (h + 1) * block_rows
                ]
        grad_query = grad_query_turned[...]
        term = ADAPTER_SCALE * dot_both(grad_query, low_q, 1, 0)
        for h in range(per_group):
            turned = term[h * LANES : (h + 1) * LANES].T
            send_upq_back[g, :, h, :] = turned[:rank]
            send_upq_back[g, :, per_group + h, :] = turned[rank:]
        grad_low_q = grad_low_q + dot_both(panel, grad_query, 1, 0)
        if g < groups - 1:
            start_all([[upq_back[g]]], n_dp)

    def of_slot(grad):
        return ADAPTER_SCALE * (
            grad[:, :rank] * in_first[:, :rank] + grad[:, rank:] * in_second[:, :rank]
        )

    grad_k, grad_v = grad_key[...], grad_value[...]
    store_packed(
        partial_back,
        jnp.concatenate(
            [of_slot(grad_low_q.T), of_slot(dot_both(grad_k, up_k, 1, 1))], axis=1
        ),
        of_slot(dot_both(grad_v, up_v, 1, 1)),
    )
    grad_sum = SumOverMp(partial_back, landed_back, total_back, sum_sems.at[1], mp, n_mp)
    term = ADAPTER_SCALE * dot_both(low_k, grad_k, 0, 0)
    send_upkv_back[:, 0, :] = term[:rank]
    send_upkv_back[:, 2, :] = term[rank:]
    term = ADAPTER_SCALE * dot_both(low_v, grad_v, 0, 0)
    send_upkv_back[:, 1, :] = term[:rank]
    send_upkv_back[:, 3, :] = term[rank:]
    grad_sum.scatter()
    start_all([[upq_back[groups - 1], upkv_back]], n_dp)
    grad_sum.gather()
    for one in [upkv_back] + upq_back:
        one.keep()
    grad_sum.arrive()
    grad_wide, grad_narrow = load_packed(total_back, row_total)
    grads = jnp.concatenate(
        [
            grad_wide * in_first,
            grad_wide * in_second,
            grad_narrow * in_first[:, :rank],
            grad_narrow * in_second[:, :rank],
        ],
        axis=1,
    )
    term = dot(rows_turned[...], jnp.concatenate(parts(grads), axis=1), 1, 0)
    for i in range(3):
        send_down_back[:, i * columns : (i + 1) * columns, :] = (
            term[:, i * LANES : (i + 1) * LANES] + term[:, (3 + i) * LANES : (4 + i) * LANES]
        ).reshape(n_dp, columns, LANES)
    start_all([[down_back]], n_dp)
    down_back.keep()

    for one in [down_in, upkv_in] + upq_in:
        one.wait_send()
    low_sum.finish()
    grad_sum.finish()
    for one in [upkv_back] + upq_back + [down_back]:
        one.wait_recv()
        one.wait_send()


def owner_kernel(down_ref, upq_ref, upkv_ref, table_ref, out_down, out_upq, out_upkv):
    tenants, columns = out_down.shape[0], out_down.shape[1]
    rank = out_down.shape[2] // 3
    groups, n_dp = upq_ref.shape[0], upq_ref.shape[1]
    per_group = upq_ref.shape[2] // 2
    tenant = lax.broadcasted_iota(jnp.int32, (tenants, n_dp), 0)
    owned = [
        jnp.where(tenant == table_ref[slot : slot + 1, :], 1.0, 0.0).astype(BF16)
        for slot in range(2)
    ]
    owned_both = jnp.concatenate(owned, axis=1)

    def owner_sum(pairs):
        terms = jnp.concatenate(
            [jnp.concatenate([a, b], axis=0) for a, b in pairs], axis=1
        )
        return dot_exact_left(owned_both, terms, 1, 0)

    def spread(ref, first, count, step, store):
        for start in range(0, count, 4):
            span = range(start, min(start + 4, count))
            total = owner_sum([(ref[:, first + r, :], ref[:, first + step + r, :]) for r in span])
            for n, r in enumerate(span):
                store(r, total[:, n * LANES : (n + 1) * LANES])

    def store_down(r, total):
        out_down[:, r, 0:LANES] = total

    spread(down_ref, 0, columns, columns, store_down)
    for start in range(0, columns, 4):
        both = jnp.concatenate(
            [down_ref[:, 2 * columns + r, :] for r in range(start, start + 4)], axis=1
        )
        of_first = dot_exact_left(owned[0], both, 1, 0)
        of_second = dot_exact_left(owned[1], both, 1, 0)
        for n in range(4):
            out_down[:, start + n, LANES : LANES + rank] = (
                of_first[:, n * LANES : n * LANES + rank]
                + of_second[:, n * LANES + rank : (n + 1) * LANES]
            )
    for g in range(groups):

        def store_upq(r, total, g=g):
            out_upq[:, g * per_group + r, :] = total

        spread(upq_ref.at[g], 0, per_group, per_group, store_upq)

    def store_upkv(r, total):
        out_upkv[:, r, :] = total

    spread(upkv_ref, 0, 2, 2, store_upkv)


def on_device(
    normed_input_rows,
    frozen_queries,
    frozen_keys,
    frozen_values,
    attention_output_gradient,
    adapter_down_weight,
    adapter_up_query,
    adapter_up_key_value,
    document_numbers,
    block_tenant_slot,
    shard_tenant_table,
    *,
    n_dp,
    n_mp,
):
    row_total = normed_input_rows.shape[0]
    tenants, columns, three_rank = adapter_down_weight.shape
    heads = frozen_queries.shape[1] // LANES
    upq = adapter_up_query.reshape(tenants, heads, LANES)
    upkv = adapter_up_key_value.reshape(tenants, 2, LANES)
    groups = 2
    table = shard_tenant_table.T
    down_shape = (n_dp, 3 * columns, LANES)
    upq_shape = (groups, n_dp, 2 * heads // groups, LANES)
    upkv_shape = (n_dp, 4, LANES)
    packed = row_total * three_rank // LANES
    vmem = pl.BlockSpec(memory_space=pltpu.VMEM)
    smem = pl.BlockSpec(memory_space=pltpu.SMEM)
    sums = [
        pltpu.VMEM((packed, LANES), F32),
        pltpu.VMEM((n_mp, packed // n_mp, LANES), F32),
        pltpu.VMEM((packed, LANES), F32),
    ]
    loaded = (
        normed_input_rows,
        frozen_queries,
        frozen_keys,
        frozen_values,
        attention_output_gradient,
        adapter_down_weight,
        upq,
        upkv,
    )
    got = pl.pallas_call(
        functools.partial(whole_kernel, n_dp, n_mp, groups),
        out_shape=[jax.ShapeDtypeStruct(s, F32) for s in (down_shape, upq_shape, upkv_shape)],
        in_specs=[pl.BlockSpec(memory_space=pl.ANY)] * 8 + [smem] * 3,
        out_specs=[vmem] * 3,
        scratch_shapes=[
            *(pltpu.VMEM(a.shape, a.dtype) for a in loaded),
            pltpu.VMEM(down_shape, F32),
            pltpu.VMEM(upq_shape, F32),
            pltpu.VMEM(upkv_shape, F32),
            pltpu.VMEM(down_shape, F32),
            pltpu.VMEM(upq_shape, F32),
            pltpu.VMEM(upkv_shape, F32),
            *sums,
            *sums,
            pltpu.VMEM(normed_input_rows.shape[::-1], BF16),
            pltpu.VMEM((row_total, row_total), F32),
            pltpu.VMEM((heads // groups * LANES, row_total), F32),
            pltpu.VMEM((row_total, LANES), F32),
            pltpu.VMEM((row_total, LANES), F32),
            pltpu.VMEM(upq_shape, F32),
            pltpu.VMEM(upkv_shape, F32),
            pltpu.VMEM(down_shape, F32),
            pltpu.SemaphoreType.DMA((len(loaded),)),
            pltpu.SemaphoreType.DMA((8 + 4 * groups, n_dp)),
            pltpu.SemaphoreType.DMA((2, 4, n_mp)),
        ],
        compiler_params=pltpu.CompilerParams(
            collective_id=0, has_side_effects=True, vmem_limit_bytes=60 * 1024 * 1024
        ),
        name="whole",
    )(*loaded, block_tenant_slot, document_numbers, table)
    grad_down, grad_upq, grad_upkv = pl.pallas_call(
        owner_kernel,
        out_shape=[
            jax.ShapeDtypeStruct(adapter_down_weight.shape, F32),
            jax.ShapeDtypeStruct(upq.shape, F32),
            jax.ShapeDtypeStruct(upkv.shape, F32),
        ],
        in_specs=[vmem] * 4,
        out_specs=[vmem] * 3,
        name="owner",
    )(*got, table)
    return (
        grad_down,
        grad_upq.reshape(adapter_up_query.shape),
        grad_upkv.reshape(adapter_up_key_value.shape),
    )


def solution(mesh):
    placed = (
        P("dp", "mp"),
        P("dp", "mp"),
        P("dp", "mp"),
        P("dp", "mp"),
        P("dp", "mp"),
        P(None, ("mp", "dp"), None),
        P(None, "dp", "mp"),
        P(None, "dp", "mp", None),
        P("dp"),
        P("dp"),
        P(),
    )
    return jax.shard_map(
        functools.partial(on_device, n_dp=mesh.shape["dp"], n_mp=mesh.shape["mp"]),
        mesh=mesh,
        in_specs=placed,
        out_specs=(P(None, ("mp", "dp"), None), P(None, "dp", "mp"), P(None, "dp", "mp", None)),
        check_vma=False,
    )
```

```python
import functools

import jax
import jax.numpy as jnp
from jax import lax
from jax.experimental import pallas as pl
from jax.experimental.pallas import tpu as pltpu
from jax.sharding import PartitionSpec as P

ADAPTER_SCALE = 0.5
MASKED = -1e30
MESH = pl.DeviceIdType.MESH
LANES = 128
DOC_ROWS = 16
PLANE = 4
F32 = jnp.float32
BF16 = jnp.bfloat16


def dot(a, b, ca, cb):
    return lax.dot_general(a, b, (((ca,), (cb,)), ((), ())), preferred_element_type=F32)


def parts(a):
    high = a.astype(BF16)
    return high, (a - high.astype(F32)).astype(BF16)


def dot_exact_left(a, b, ca, cb):
    high, low = parts(b)
    return dot(a, high, ca, cb) + dot(a, low, ca, cb)


def dot_both(a, b, ca, cb):
    a_high, a_low = parts(a)
    b_high, b_low = parts(b)
    return dot(a_high, b_high, ca, cb) + (dot(a_high, b_low, ca, cb) + dot(a_low, b_high, ca, cb))


def signal(sem, **device):
    pl.semaphore_signal(sem, inc=1, device_id=device, device_id_type=MESH)


class Place:
    def __init__(self, n_dp, n_mp):
        self.n_dp, self.n_mp = n_dp, n_mp
        self.planes = n_dp // PLANE
        self.per = self.planes // n_mp
        self.dp, self.mp = lax.axis_index("dp"), lax.axis_index("mp")
        self.z, self.q = lax.div(self.dp, PLANE), lax.rem(self.dp, PLANE)
        self.worker_slot = lax.div(self.z, n_mp)
        self.is_own_worker = self.worker_mp(self.z) == self.mp

    def worker_mp(self, z):
        return lax.rem(self.z + z, self.n_mp)

    def worker(self, dz):
        z = lax.rem(self.z + dz, self.planes)
        return z, {"dp": z * PLANE + self.q, "mp": self.worker_mp(z)}

    def served_z(self, w, m):
        return lax.rem(m + self.planes - self.z, self.n_mp) + w * self.n_mp

    def served(self, w, m=None, q=None):
        m, q = (self.mp, self.q) if m is None else (m, q)
        return self.served_z(w, m) * PLANE + q

    def serves_own_plane(self, w):
        return self.served_z(w, self.mp) == self.z

    def mate(self, k, sign):
        dq, dm = lax.div(k, self.n_mp), lax.rem(k, self.n_mp)
        q = lax.rem(self.q + PLANE + sign * dq, PLANE)
        m = lax.rem(self.mp + self.n_mp + sign * dm, self.n_mp)
        return q, m


def barrier(at):
    sem = pltpu.get_barrier_semaphore()

    @pl.loop(1, at.n_dp)
    def _(k):
        signal(sem, dp=lax.rem(at.dp + k, at.n_dp))

    for k in range(1, at.n_mp):
        signal(sem, mp=lax.rem(at.mp + k, at.n_mp))

    @pl.loop(at.n_mp, PLANE * at.n_mp)
    def _(k):
        q, m = at.mate(k, 1)

        @pl.when(m != at.mp)
        def _():
            signal(sem, dp=at.z * PLANE + q, mp=m)

    @pl.loop(1, at.planes)
    def _(dz):
        _, device = at.worker(dz)
        signal(sem, **device)

    for w in range(at.per):

        @pl.when(jnp.logical_not(at.serves_own_plane(w)))
        def _():
            @pl.loop(0, at.n_mp)
            def _(m):
                signal(sem, dp=at.served(w), mp=m)

    count = (at.n_dp - 1) + (at.n_mp - 1) + (PLANE - 1) * (at.n_mp - 1) + (at.planes - 1)
    count = count + at.n_mp * at.per - jnp.where(at.is_own_worker, at.n_mp, 0)
    return lambda: pl.semaphore_wait(sem, count)


def remote(source, target, send, recv, **device):
    return pltpu.make_async_remote_copy(
        src_ref=source,
        dst_ref=target,
        send_sem=send,
        recv_sem=recv,
        device_id=device,
        device_id_type=MESH,
    )


class ToWorkers:
    def __init__(self, at, source, target, send, recv, same):
        self.at, self.source, self.target, self.send, self.recv = at, source, target, send, recv
        self.same = same

    def copy(self, dz):
        z, device = self.at.worker(dz)
        source = self.source if self.same else self.source.at[z]
        slot = (self.at.worker_slot, self.at.mp)
        return remote(source, self.target.at[slot], self.send.at[dz], self.recv.at[slot], **device)

    def start(self):
        at = self.at

        @pl.loop(1, at.planes)
        def _(dz):
            self.copy(dz).start()

        @pl.when(jnp.logical_not(at.is_own_worker))
        def _():
            self.copy(0).start()

        @pl.when(at.is_own_worker)
        def _():
            self.target[at.worker_slot, at.mp] = (
                self.source[...] if self.same else self.source[at.z]
            )

    def wait_recv(self):
        at = self.at
        for w in range(at.per):

            @pl.loop(0, at.n_mp)
            def _(m):
                @pl.when(jnp.logical_not(at.serves_own_plane(w) & (m == at.mp)))
                def _():
                    place = self.target.at[w, m]
                    remote(
                        place, place, self.send.at[0], self.recv.at[w, m], dp=at.served(w), mp=m
                    ).wait_recv()

    def wait_send(self):
        @pl.loop(1, self.at.planes)
        def _(dz):
            self.copy(dz).wait_send()

        @pl.when(jnp.logical_not(self.at.is_own_worker))
        def _():
            self.copy(0).wait_send()


class FromWorkers:
    def __init__(self, at, source, target, send, recv):
        self.at, self.source, self.target, self.send, self.recv = at, source, target, send, recv

    def copy(self, w, m):
        at = self.at
        return remote(
            self.source.at[w, m],
            self.target.at[at.z],
            self.send.at[w, m],
            self.recv.at[at.z],
            dp=at.served(w),
            mp=m,
        )

    def each(self, act):
        at = self.at
        for w in range(at.per):

            @pl.loop(0, at.n_mp)
            def _(m):
                @pl.when(jnp.logical_not(at.serves_own_plane(w) & (m == at.mp)))
                def _():
                    act(self.copy(w, m))

    def start(self):
        at = self.at
        self.each(lambda copy: copy.start())

        @pl.when(at.is_own_worker)
        def _():
            self.target[at.z] = self.source[at.worker_slot, at.mp]

    def wait_recv(self):
        at = self.at

        @pl.loop(0, at.planes)
        def _(z):
            @pl.when(jnp.logical_not(at.is_own_worker & (z == at.z)))
            def _():
                place = self.target.at[z]
                remote(
                    place,
                    place,
                    self.send.at[0, 0],
                    self.recv.at[z],
                    dp=z * PLANE + at.q,
                    mp=at.worker_mp(z),
                ).wait_recv()

    def wait_send(self):
        self.each(lambda copy: copy.wait_send())


class InPlane:
    def __init__(self, at, pick, place, send, recv):
        self.at, self.pick, self.place, self.send, self.recv = at, pick, place, send, recv

    def copy(self, k, w, sign):
        at = self.at
        q, m = at.mate(k, sign)
        target = self.place(w, at.mp, at.q) if sign == 1 else self.place(w, m, q)
        source = self.pick(w, m, q) if sign == 1 else target
        return remote(
            source, target, self.send.at[k, w], self.recv.at[k, w], dp=at.z * PLANE + q, mp=m
        )

    def each(self, sign, act):
        @pl.loop(1, PLANE * self.at.n_mp)
        def _(k):
            for w in range(self.at.per):
                act(self.copy(k, w, sign))

    def start(self):
        self.each(1, lambda copy: copy.start())

    def keep(self):
        at = self.at
        for w in range(at.per):
            self.place(w, at.mp, at.q)[...] = self.pick(w, at.mp, at.q)[...]

    def wait_recv(self):
        self.each(-1, lambda copy: copy.wait_recv())

    def wait_send(self):
        self.each(1, lambda copy: copy.wait_send())


class Announce:
    def __init__(self, at, ref, send, recv):
        self.at, self.ref, self.send, self.recv = at, ref, send, recv

    def copy(self, k, sign):
        at = self.at
        peer = lax.rem(at.dp + at.n_dp + sign * k, at.n_dp)
        place = self.ref.at[at.dp if sign == 1 else peer]
        return remote(place, place, self.send.at[k], self.recv.at[k], dp=peer)

    def each(self, sign, act):
        @pl.loop(1, self.at.n_dp)
        def _(k):
            act(self.copy(k, sign))

    def start(self):
        self.each(1, lambda copy: copy.start())

    def wait_recv(self):
        self.each(-1, lambda copy: copy.wait_recv())

    def wait_send(self):
        self.each(1, lambda copy: copy.wait_send())


class Exchange:
    def __init__(self, source, target, send, recv, dp, n_dp):
        self.source, self.target, self.send, self.recv = source, target, send, recv
        self.dp, self.n_dp = dp, n_dp

    def piece(self, k, peer, slot):
        return pltpu.make_async_remote_copy(
            src_ref=self.source.at[peer],
            dst_ref=self.target.at[slot],
            send_sem=self.send.at[k],
            recv_sem=self.recv.at[k],
            device_id={"dp": peer},
            device_id_type=MESH,
        )

    def start(self, k):
        self.piece(k, lax.rem(self.dp + k, self.n_dp), self.dp).start()

    def keep(self):
        self.target[pl.ds(self.dp, 1)] = self.source[pl.ds(self.dp, 1)]

    def wait_recv(self):
        @pl.loop(1, self.n_dp)
        def _(k):
            origin = lax.rem(self.dp + self.n_dp - k, self.n_dp)
            self.piece(k, origin, origin).wait_recv()

    def wait_send(self):
        @pl.loop(1, self.n_dp)
        def _(k):
            self.piece(k, lax.rem(self.dp + k, self.n_dp), self.dp).wait_send()


def start_all(exchanges, n_dp):
    for group in exchanges:

        @pl.loop(0, n_dp - 1)
        def _(i):
            half = lax.div(i + 2, 2)
            k = jnp.where(lax.rem(i, 2) == 0, half, n_dp - half)
            for exchange in group:
                exchange.start(k)


class SumOverMp:
    def __init__(self, at, partial, landed, total, sems):
        self.at, self.partial, self.landed, self.total, self.sems = at, partial, landed, total, sems

    def scatter_copy(self, k):
        peer = lax.rem(self.at.mp + k, self.at.n_mp)
        return remote(
            self.partial.at[peer], self.landed.at[k], self.sems.at[0, k], self.sems.at[1, k], mp=peer
        )

    def spread_copy(self, k, sign):
        at = self.at
        peer = lax.rem(at.mp + at.n_mp + sign * k, at.n_mp)
        place = self.total.at[at.mp if sign == 1 else peer]
        return remote(place, place, self.sems.at[2, k], self.sems.at[3, k], mp=peer)

    def scatter(self):
        for k in range(1, self.at.n_mp):
            self.scatter_copy(k).start()

    def summed(self):
        mine = self.partial[self.at.mp]
        for k in range(1, self.at.n_mp):
            self.scatter_copy(k).wait_recv()
            mine = mine + self.landed[k]
        return mine

    def spread(self, mine):
        self.total[self.at.mp] = mine
        for k in range(1, self.at.n_mp):
            self.spread_copy(k, 1).start()

    def arrive(self):
        for k in range(1, self.at.n_mp):
            self.spread_copy(k, -1).wait_recv()

    def wait_send(self):
        for k in range(1, self.at.n_mp):
            self.scatter_copy(k).wait_send()
            self.spread_copy(k, 1).wait_send()


def side_by_side(a):
    half = a.shape[-2] // 2
    return jnp.concatenate([a[..., :half, :], a[..., half:, :]], axis=-1)


def one_below_other(a):
    half = a.shape[-1] // 2
    return jnp.concatenate([a[..., :half], a[..., half:]], axis=-2)


def pack(a, wide):
    return jnp.concatenate([a[..., :wide], side_by_side(a[..., wide:])], axis=-2)


def unpack(a):
    rows = a.shape[-2] * 2 // 3
    return jnp.concatenate([a[..., :rows, :], one_below_other(a[..., rows:, :])], axis=-1)


def by_devices(a, columns, wide):
    return pack(a.reshape(a.shape[0] // columns, columns, a.shape[1]), wide)


def from_devices(a):
    a = unpack(a)
    return a.reshape(a.shape[0] * a.shape[1], a.shape[2])


def whole_kernel(
    n_dp,
    n_mp,
    rows_hbm,
    queries_hbm,
    keys_hbm,
    values_hbm,
    upstream_hbm,
    down_hbm,
    upq_hbm,
    upkv_hbm,
    slot_ref,
    doc_ref,
    table_ref,
    got_one,
    got_two,
    got_up_a,
    got_up_b,
    flags,
    rows_ref,
    queries_ref,
    keys_ref,
    values_ref,
    upstream_ref,
    down_ref,
    upq_ref,
    upkv_ref,
    send_panels,
    recv_panels,
    send_rows,
    recv_rows,
    send_part,
    recv_part,
    send_two,
    recv_two,
    send_up_a,
    send_up_b,
    recv_up_a,
    recv_up_b,
    partial,
    landed,
    total,
    partial_back,
    landed_back,
    total_back,
    low_one_back,
    recv_low,
    served_rows_turned,
    rows_turned,
    bias,
    grad_query_turned,
    grad_key,
    grad_value,
    send_up_a_back,
    send_up_b_back,
    send_two_back,
    send_one_back,
    load_sems,
    peer_sems,
    plane_sems,
    plane_sems_back,
    to_sems,
    to_sems_recv,
    from_sems,
    from_sems_recv,
    sum_sems,
):
    at = Place(n_dp, n_mp)
    dp = at.dp
    row_total, width = rows_ref.shape
    rank = down_ref.shape[2] // 3
    wide = 2 * rank
    columns = down_ref.shape[1]
    heads = queries_ref.shape[1] // LANES
    per_group = heads // 2
    group_lanes = per_group * LANES
    blocks = slot_ref.shape[0]
    block_rows = row_total // blocks
    plane_columns = width // at.planes
    inverse = 1.0 / float(LANES) ** 0.5

    loads = [
        pltpu.make_async_copy(source, target, load_sems.at[i])
        for i, (source, target) in enumerate(
            [
                (down_hbm, down_ref),
                (upq_hbm, upq_ref),
                (upkv_hbm, upkv_ref),
                (rows_hbm, rows_ref),
                (keys_hbm, keys_ref),
                (values_hbm, values_ref),
                (queries_hbm, queries_ref),
                (upstream_hbm, upstream_ref),
            ]
        )
    ]
    for load in loads:
        load.start()
    arrived = barrier(at)

    late = slot_ref[1].astype(F32)
    early = 1.0 - late
    flags[pl.ds(dp, 1)] = jnp.full((1, 1, LANES), late)
    for load in loads[:4]:
        load.wait()
    rows = rows_ref[...]
    outer_first = rows[:block_rows].astype(F32)
    outer_last = rows[row_total - block_rows :].astype(F32)
    rows_one = outer_first * late + outer_last * early
    for z in range(0, at.planes, 2):
        tile = rows_one[:, z * plane_columns : (z + 2) * plane_columns]
        send_rows[z] = side_by_side(tile[:, :plane_columns])
        send_rows[z + 1] = side_by_side(tile[:, plane_columns:])

    @pl.loop(0, n_dp)
    def _(d):
        first, second = table_ref[0, d], table_ref[1, d]
        a, b = down_ref[first], down_ref[second]
        send_panels[d] = jnp.concatenate(
            [a[:, :wide], b[:, :wide], jnp.concatenate([a[:, wide:], b[:, wide:]], axis=1)],
            axis=0,
        )
        a, b = upq_ref[first], upq_ref[second]
        send_up_a[d, 0] = a[:per_group]
        send_up_a[d, 1] = b[:per_group]
        send_up_a[d, 2] = jnp.concatenate([upkv_ref[first], upkv_ref[second]], axis=0)
        send_up_b[d, 0] = a[per_group:]
        send_up_b[d, 1] = b[per_group:]

    arrived()

    def exchange(index, source, target):
        return Exchange(
            source, target, peer_sems.at[2 * index], peer_sems.at[2 * index + 1], dp, n_dp
        )

    announce = Announce(at, flags, peer_sems.at[0], peer_sems.at[1])
    two_in = exchange(1, send_two, recv_two)
    up_a_in = exchange(2, send_up_a, recv_up_a)
    up_b_in = exchange(3, send_up_b, recv_up_b)
    two_back = exchange(4, send_two_back, got_two)
    up_a_back = exchange(5, send_up_a_back, got_up_a)
    up_b_back = exchange(6, send_up_b_back, got_up_b)
    rows_out = ToWorkers(at, send_rows, recv_rows, to_sems.at[0], to_sems_recv.at[0], False)
    low_out = ToWorkers(at, low_one_back, recv_low, to_sems.at[1], to_sems_recv.at[1], True)
    part_back = FromWorkers(at, send_part, recv_part, from_sems, from_sems_recv)
    panels_in = InPlane(
        at,
        lambda w, m, q: send_panels.at[at.served(w, m, q)],
        lambda w, m, q: recv_panels.at[w, m, q],
        plane_sems.at[0],
        plane_sems.at[1],
    )
    one_back = InPlane(
        at,
        lambda w, m, q: send_one_back.at[w, m, q],
        lambda w, m, q: got_one.at[at.served(w, m, q)],
        plane_sems_back.at[0],
        plane_sems_back.at[1],
    )
    announce.start()
    rows_out.start()
    panels_in.start()
    panels_in.keep()

    rows_two = jnp.concatenate(
        [
            (outer_last * late + outer_first * early).astype(BF16),
            rows[block_rows : row_total - block_rows],
        ],
        axis=0,
    )
    announce.wait_recv()

    @pl.loop(0, n_dp)
    def _(d):
        second = flags[d]
        first = 1.0 - second
        panel = send_panels[d]
        narrow = panel[2 * columns :]
        narrow = narrow[:, :rank] * first[:, :rank] + narrow[:, rank:] * second[:, :rank]
        send_two[d] = jnp.concatenate(
            [
                panel[:columns] * first + panel[columns : 2 * columns] * second,
                side_by_side(narrow),
            ],
            axis=0,
        )

    start_all([[two_in]], n_dp)
    two_in.keep()
    rows_turned[...] = rows_two.T

    lane = lax.broadcasted_iota(jnp.int32, (1, row_total), 1)
    doc_lane = jnp.zeros((1, row_total), jnp.int32)
    for start in range(0, row_total, DOC_ROWS):
        doc_lane = jnp.where(lane >= start, doc_ref[start], doc_lane)
    sub = lax.broadcasted_iota(jnp.int32, (DOC_ROWS, row_total), 0)
    for start in range(0, row_total, DOC_ROWS):
        joined = (doc_lane == doc_ref[start]) & (sub + start <= lane)
        bias[start : start + DOC_ROWS] = jnp.where(joined, 0.0, MASKED).astype(F32)
    in_second = jnp.concatenate(
        [jnp.full((block_rows, LANES), slot_ref[b].astype(F32)) for b in range(blocks)], axis=0
    )
    in_first = 1.0 - in_second

    rows_out.wait_recv()
    panels_in.wait_recv()
    for w in range(at.per):
        served = jnp.concatenate(
            [one_below_other(recv_rows[w, m]) for m in range(n_mp)], axis=1
        ).astype(BF16)
        served_rows_turned[w] = served.T
        panels = jnp.concatenate(
            [
                recv_panels[w, :, :, i * columns : (i + 1) * columns, :].reshape(
                    n_mp * PLANE * columns, LANES
                )
                for i in range(3)
            ],
            axis=1,
        )
        low = dot(served, jnp.concatenate(parts(panels), axis=1), 1, 0)
        low = low[:, : 3 * LANES] + low[:, 3 * LANES :]
        first = flags[at.served(w)]
        second = 1.0 - first
        both = low[:, 2 * LANES :]
        low = jnp.concatenate(
            [
                low[:, :LANES] * first + low[:, LANES : 2 * LANES] * second,
                both[:, :rank] * first[:, :rank] + both[:, rank:] * second[:, :rank],
            ],
            axis=1,
        )
        low = pack(low, wide)
        send_part[w] = low.reshape(n_mp, low.shape[0] // n_mp, LANES)
    part_back.start()
    start_all([[up_a_in], [up_b_in]], n_dp)
    up_a_in.keep()
    up_b_in.keep()
    for load in loads[4:]:
        load.wait()

    two_in.wait_recv()
    low = dot(rows_two, jnp.concatenate(parts(from_devices(recv_two[...])), axis=1), 1, 0)
    low = pack(low[:, : 3 * rank] + low[:, 3 * rank :], wide)
    partial[...] = low.reshape(partial.shape)
    low_sum = SumOverMp(at, partial, landed, total, sum_sems.at[0])
    low_sum.scatter()
    part_back.wait_recv()
    mine_one = recv_part[0]
    for z in range(1, at.planes):
        mine_one = mine_one + recv_part[z]
    two_rows = partial.shape[1]
    one_rows = mine_one.shape[0]
    low_sum.spread(jnp.concatenate([low_sum.summed(), mine_one], axis=0))
    low_sum.arrive()
    low_two = unpack(total[:, :two_rows].reshape(n_mp * two_rows, LANES))
    low_one = unpack(total[:, two_rows:].reshape(n_mp * one_rows, LANES))
    low = jnp.concatenate(
        [
            low_one * late + low_two[:block_rows] * early,
            low_two[block_rows:],
            low_two[:block_rows] * late + low_one * early,
        ],
        axis=0,
    )

    def by_slot(low):
        return jnp.concatenate(
            [low * in_first[:, :rank], low * in_second[:, :rank]], axis=1
        )

    low_q = by_slot(low[:, :rank])
    low_k = by_slot(low[:, rank:wide])
    low_v = by_slot(low[:, wide:])

    def adapted(frozen, low, panel):
        return (frozen.astype(F32) + ADAPTER_SCALE * dot_both(low, panel, 1, 0)).astype(BF16)

    up_a_in.wait_recv()
    up_k = jnp.concatenate([recv_up_a[:, 2, 0, :], recv_up_a[:, 2, 2, :]], axis=0)
    up_v = jnp.concatenate([recv_up_a[:, 2, 1, :], recv_up_a[:, 2, 3, :]], axis=0)
    key = adapted(keys_ref[...], low_k, up_k)
    value = adapted(values_ref[...], low_v, up_v)
    key_turned = key.T
    grad_key[...] = jnp.zeros_like(grad_key)
    grad_value[...] = jnp.zeros_like(grad_value)
    grad_low_q = jnp.zeros((wide, row_total), F32)
    for g, recv_up, send_back in ((0, recv_up_a, send_up_a_back), (1, recv_up_b, send_up_b_back)):
        lanes = slice(g * group_lanes, (g + 1) * group_lanes)
        if g == 1:
            up_b_in.wait_recv()
        panel = jnp.concatenate(
            [
                jnp.concatenate([recv_up[:, 0, h, :], recv_up[:, 1, h, :]], axis=0)
                for h in range(per_group)
            ],
            axis=1,
        )
        query = adapted(queries_ref[:, lanes], low_q, panel)
        upstream = upstream_ref[:, lanes]

        def stacked(a, first):
            return jnp.concatenate(
                [
                    a[first : first + block_rows, h * LANES : (h + 1) * LANES]
                    for h in range(per_group)
                ],
                axis=0,
            )

        for b in range(blocks):
            first, last = b * block_rows, (b + 1) * block_rows
            query_b, upstream_b = stacked(query, first), stacked(upstream, first)
            mask = jnp.concatenate([bias[0:last, first:last]] * per_group, axis=1)
            scores = dot(key[:last], query_b, 1, 1) * inverse + mask
            weights = jnp.exp(scores - jnp.max(scores, axis=0, keepdims=True))
            probs = weights * (1.0 / jnp.sum(weights, axis=0, keepdims=True))
            grad_probs = dot(value[:last], upstream_b, 1, 1)
            inner = jnp.sum(probs * grad_probs, axis=0, keepdims=True)
            grad_scores = (probs * (grad_probs - inner) * inverse).astype(BF16)
            grad_key[0:last] += dot(grad_scores, query_b, 1, 0)
            grad_value[0:last] += dot(probs.astype(BF16), upstream_b, 1, 0)
            turned = dot(key_turned[:, :last], grad_scores, 1, 0)
            for h in range(per_group):
                grad_query_turned[h * LANES : (h + 1) * LANES, first:last] = turned[
                    :, h * block_rows : (h + 1) * block_rows
                ]
        grad_query = grad_query_turned[...]
        term = ADAPTER_SCALE * dot_both(grad_query, low_q, 1, 0)
        for h in range(per_group):
            turned = term[h * LANES : (h + 1) * LANES].T
            send_back[:, 0, h, :] = turned[:rank]
            send_back[:, 1, h, :] = turned[rank:]
        grad_low_q = grad_low_q + dot_both(panel, grad_query, 1, 0)
        if g == 0:
            start_all([[up_a_back]], n_dp)

    def of_slot(grad):
        return ADAPTER_SCALE * (
            grad[:, :rank] * in_first[:, :rank] + grad[:, rank:] * in_second[:, :rank]
        )

    grad_k, grad_v = grad_key[...], grad_value[...]
    grad_low = jnp.concatenate(
        [
            of_slot(grad_low_q.T),
            of_slot(dot_both(grad_k, up_k, 1, 1)),
            of_slot(dot_both(grad_v, up_v, 1, 1)),
        ],
        axis=1,
    )
    outer_first = grad_low[:block_rows]
    outer_last = grad_low[row_total - block_rows :]
    grad_one = pack(outer_first * late + outer_last * early, wide)
    grad_two = pack(
        jnp.concatenate(
            [
                outer_last * late + outer_first * early,
                grad_low[block_rows : row_total - block_rows],
            ],
            axis=0,
        ),
        wide,
    )
    partial_back[...] = jnp.concatenate(
        [grad_two.reshape(n_mp, two_rows, LANES), grad_one.reshape(n_mp, one_rows, LANES)],
        axis=1,
    )
    grad_sum = SumOverMp(at, partial_back, landed_back, total_back, sum_sems.at[1])
    term = ADAPTER_SCALE * dot_both(low_k, grad_k, 0, 0)
    send_up_b_back[:, 2, 0, :] = term[:rank]
    send_up_b_back[:, 2, 2, :] = term[rank:]
    term = ADAPTER_SCALE * dot_both(low_v, grad_v, 0, 0)
    send_up_b_back[:, 2, 1, :] = term[:rank]
    send_up_b_back[:, 2, 3, :] = term[rank:]
    grad_sum.scatter()
    start_all([[up_b_back]], n_dp)
    mine = grad_sum.summed()
    low_one_back[...] = mine[two_rows:]
    grad_sum.spread(mine[:two_rows])
    low_out.start()
    up_a_back.keep()
    up_b_back.keep()
    grad_sum.arrive()
    grads = unpack(total_back[...].reshape(n_mp * two_rows, LANES))
    term = dot(rows_turned[...], jnp.concatenate(parts(grads), axis=1), 1, 0)
    send_two_back[...] = by_devices(term[:, : 3 * rank] + term[:, 3 * rank :], columns, wide)
    start_all([[two_back]], n_dp)
    two_back.keep()

    low_out.wait_recv()
    for w in range(at.per):
        grads = unpack(recv_low[w].reshape(n_mp * one_rows, LANES))
        term = dot(served_rows_turned[w], jnp.concatenate(parts(grads), axis=1), 1, 0)
        term = by_devices(term[:, : 3 * rank] + term[:, 3 * rank :], columns, wide)
        send_one_back[w] = term.reshape(n_mp, PLANE, term.shape[1], LANES)
    one_back.start()
    one_back.keep()

    for one in (
        announce,
        rows_out,
        panels_in,
        two_in,
        part_back,
        up_a_in,
        up_b_in,
        low_sum,
        grad_sum,
        low_out,
    ):
        one.wait_send()
    for one in (up_a_back, up_b_back, one_back, two_back):
        one.wait_recv()
        one.wait_send()


def owner_kernel(
    one_ref, two_ref, up_a_ref, up_b_ref, flags_ref, table_ref, out_down, out_upq, out_upkv
):
    tenants, columns = out_down.shape[0], out_down.shape[1]
    rank = out_down.shape[2] // 3
    n_dp = one_ref.shape[0]
    per_group = up_a_ref.shape[2]
    tenant = lax.broadcasted_iota(jnp.int32, (tenants, n_dp), 0)
    owned = [
        jnp.where(tenant == table_ref[slot : slot + 1, :], 1.0, 0.0).astype(F32)
        for slot in range(2)
    ]
    late = flags_ref[:, 0, :].T[0:1, :]
    early = 1.0 - late
    owned_down = jnp.concatenate(
        [owned[0] * late + owned[1] * early, owned[1] * late + owned[0] * early], axis=1
    ).astype(BF16)
    owned_up = jnp.concatenate(owned, axis=1).astype(BF16)

    def spread(hot, count, pair, store):
        for start in range(0, count, 4):
            span = range(start, min(start + 4, count))
            terms = jnp.concatenate(
                [jnp.concatenate(pair(r), axis=0) for r in span], axis=1
            )
            total = dot_exact_left(hot, terms, 1, 0)
            for n, r in enumerate(span):
                store(r, total[:, n * LANES : (n + 1) * LANES])

    def store_down(r, total):
        if r < columns:
            out_down[:, r, 0:LANES] = total
        else:
            out_down[:, r - columns, LANES : LANES + rank] = total[:, :rank]
            out_down[:, r - columns // 2, LANES : LANES + rank] = total[:, rank:]

    spread(
        owned_down, one_ref.shape[1], lambda r: [one_ref[:, r, :], two_ref[:, r, :]], store_down
    )
    for g, ref in ((0, up_a_ref), (1, up_b_ref)):

        def store_upq(r, total, g=g):
            out_upq[:, g * per_group + r, :] = total

        spread(owned_up, per_group, lambda r, ref=ref: [ref[:, 0, r, :], ref[:, 1, r, :]], store_upq)

    def store_upkv(r, total):
        out_upkv[:, r, :] = total

    spread(owned_up, 2, lambda r: [up_b_ref[:, 2, r, :], up_b_ref[:, 2, 2 + r, :]], store_upkv)


def on_device(
    normed_input_rows,
    frozen_queries,
    frozen_keys,
    frozen_values,
    attention_output_gradient,
    adapter_down_weight,
    adapter_up_query,
    adapter_up_key_value,
    document_numbers,
    block_tenant_slot,
    shard_tenant_table,
    *,
    n_dp,
    n_mp,
):
    row_total = normed_input_rows.shape[0]
    tenants, columns, three_rank = adapter_down_weight.shape
    heads = frozen_queries.shape[1] // LANES
    upq = adapter_up_query.reshape(tenants, heads, LANES)
    upkv = adapter_up_key_value.reshape(tenants, 2, LANES)
    table = shard_tenant_table.T
    vmem = pl.BlockSpec(memory_space=pltpu.VMEM)
    smem = pl.BlockSpec(memory_space=pltpu.SMEM)
    loaded = (
        normed_input_rows,
        frozen_queries,
        frozen_keys,
        frozen_values,
        attention_output_gradient,
        adapter_down_weight,
        upq,
        upkv,
    )
    width = normed_input_rows.shape[1]
    block_rows = row_total // block_tenant_slot.shape[0]
    planes = n_dp // PLANE
    per = planes // n_mp
    one_rows = block_rows * three_rank // LANES // n_mp
    two_rows = 2 * one_rows
    all_rows = one_rows + two_rows
    piece = columns * three_rank // LANES
    send_rows_shape = (planes, block_rows * (width // planes) // LANES, LANES)

    def f32(*shape):
        return pltpu.VMEM(shape, F32)

    def dma(*shape):
        return pltpu.SemaphoreType.DMA(shape)

    outs = [
        (n_dp, piece, LANES),
        (n_dp, piece, LANES),
        (n_dp, 2, heads // 2, LANES),
        (n_dp, 3, heads // 2, LANES),
        (n_dp, 1, LANES),
    ]
    got = pl.pallas_call(
        functools.partial(whole_kernel, n_dp, n_mp),
        out_shape=[jax.ShapeDtypeStruct(s, F32) for s in outs],
        in_specs=[pl.BlockSpec(memory_space=pl.ANY)] * 8 + [smem] * 3,
        out_specs=[vmem] * len(outs),
        scratch_shapes=[
            *(pltpu.VMEM(a.shape, a.dtype) for a in loaded),
            f32(n_dp, 3 * columns, LANES),
            f32(per, n_mp, PLANE, 3 * columns, LANES),
            f32(*send_rows_shape),
            f32(per, n_mp, *send_rows_shape[1:]),
            f32(per, n_mp, one_rows, LANES),
            f32(planes, one_rows, LANES),
            f32(n_dp, piece, LANES),
            f32(n_dp, piece, LANES),
            f32(n_dp, 3, heads // 2, LANES),
            f32(n_dp, 2, heads // 2, LANES),
            f32(n_dp, 3, heads // 2, LANES),
            f32(n_dp, 2, heads // 2, LANES),
            f32(n_mp, two_rows, LANES),
            f32(n_mp, two_rows, LANES),
            f32(n_mp, all_rows, LANES),
            f32(n_mp, all_rows, LANES),
            f32(n_mp, all_rows, LANES),
            f32(n_mp, two_rows, LANES),
            f32(one_rows, LANES),
            f32(per, n_mp, one_rows, LANES),
            pltpu.VMEM((per, n_mp * PLANE * columns, block_rows), BF16),
            pltpu.VMEM((width, row_total - block_rows), BF16),
            f32(row_total, row_total),
            f32(heads // 2 * LANES, row_total),
            f32(row_total, LANES),
            f32(row_total, LANES),
            f32(n_dp, 2, heads // 2, LANES),
            f32(n_dp, 3, heads // 2, LANES),
            f32(n_dp, piece, LANES),
            f32(per, n_mp, PLANE, piece, LANES),
            dma(len(loaded)),
            dma(14, n_dp),
            dma(2, PLANE * n_mp, per),
            dma(2, PLANE * n_mp, per),
            dma(2, planes),
            dma(2, per, n_mp),
            dma(per, n_mp),
            dma(planes),
            dma(2, 4, n_mp),
        ],
        compiler_params=pltpu.CompilerParams(
            collective_id=0, has_side_effects=True, vmem_limit_bytes=60 * 1024 * 1024
        ),
        name="whole",
    )(*loaded, block_tenant_slot, document_numbers, table)
    grad_down, grad_upq, grad_upkv = pl.pallas_call(
        owner_kernel,
        out_shape=[
            jax.ShapeDtypeStruct(adapter_down_weight.shape, F32),
            jax.ShapeDtypeStruct(upq.shape, F32),
            jax.ShapeDtypeStruct(upkv.shape, F32),
        ],
        in_specs=[vmem] * 6,
        out_specs=[vmem] * 3,
        name="owner",
    )(*got, table)
    return (
        grad_down,
        grad_upq.reshape(adapter_up_query.shape),
        grad_upkv.reshape(adapter_up_key_value.shape),
    )


def solution(mesh):
    placed = (
        P("dp", "mp"),
        P("dp", "mp"),
        P("dp", "mp"),
        P("dp", "mp"),
        P("dp", "mp"),
        P(None, ("mp", "dp"), None),
        P(None, "dp", "mp"),
        P(None, "dp", "mp", None),
        P("dp"),
        P("dp"),
        P(),
    )
    return jax.shard_map(
        functools.partial(on_device, n_dp=mesh.shape["dp"], n_mp=mesh.shape["mp"]),
        mesh=mesh,
        in_specs=placed,
        out_specs=(P(None, ("mp", "dp"), None), P(None, "dp", "mp"), P(None, "dp", "mp", None)),
        check_vma=False,
    )
```

```python
import functools

import jax
import jax.numpy as jnp
from jax import lax
from jax.experimental import pallas as pl
from jax.experimental.pallas import tpu as pltpu
from jax.sharding import PartitionSpec as P

ADAPTER_SCALE = 0.5
MASKED = -1e30
MESH = pl.DeviceIdType.MESH
LANES = 128
DOC_ROWS = 16
PLANE = 4
F32 = jnp.float32
BF16 = jnp.bfloat16


def dot(a, b, ca, cb):
    return lax.dot_general(a, b, (((ca,), (cb,)), ((), ())), preferred_element_type=F32)


def parts(a):
    high = a.astype(BF16)
    return high, (a - high.astype(F32)).astype(BF16)


def dot_exact_left(a, b, ca, cb):
    high, low = parts(b)
    return dot(a, high, ca, cb) + dot(a, low, ca, cb)


def dot_both(a, b, ca, cb):
    a_high, a_low = parts(a)
    b_high, b_low = parts(b)
    return dot(a_high, b_high, ca, cb) + (dot(a_high, b_low, ca, cb) + dot(a_low, b_high, ca, cb))


def wrap(x, n):
    return jnp.where(x >= n, x - n, x)


def signal(sem, **device):
    pl.semaphore_signal(sem, inc=1, device_id=device, device_id_type=MESH)


class Place:
    def __init__(self, n_dp, n_mp):
        self.n_dp, self.n_mp = n_dp, n_mp
        self.planes = n_dp // PLANE
        self.per = self.planes // n_mp
        self.dp, self.mp = lax.axis_index("dp"), lax.axis_index("mp")
        self.z, self.q = lax.div(self.dp, PLANE), lax.rem(self.dp, PLANE)
        self.worker_slot = lax.div(self.z, n_mp)
        self.z_mp = lax.rem(self.z, n_mp)
        self.is_own_worker = self.worker_mp(self.z) == self.mp

    def worker_mp(self, z):
        return wrap(self.z_mp + wrap(z, self.n_mp), self.n_mp)

    def worker(self, dz):
        z = wrap(self.z + dz, self.planes)
        return z, {"dp": z * PLANE + self.q, "mp": self.worker_mp(z)}

    def served_z(self, w, m):
        return wrap(m + self.n_mp - self.z_mp, self.n_mp) + w * self.n_mp

    def served(self, w, m=None, q=None):
        m, q = (self.mp, self.q) if m is None else (m, q)
        return self.served_z(w, m) * PLANE + q

    def serves_own_plane(self, w):
        return self.served_z(w, self.mp) == self.z

    def mate(self, dq, dm, sign):
        if sign == 1:
            return wrap(self.q + dq, PLANE), wrap(self.mp + dm, self.n_mp)
        return wrap(self.q + PLANE - dq, PLANE), wrap(self.mp + self.n_mp - dm, self.n_mp)

    def mates(self, act):
        for dq in range(PLANE):

            @pl.loop(1 if dq == 0 else 0, self.n_mp)
            def _(dm):
                act(dq, dm)


def barrier(at):
    sem = pltpu.get_barrier_semaphore()

    @pl.loop(1, at.n_dp)
    def _(k):
        signal(sem, dp=wrap(at.dp + k, at.n_dp))

    for k in range(1, at.n_mp):
        signal(sem, mp=wrap(at.mp + k, at.n_mp))

    for dq in range(1, PLANE):

        @pl.loop(1, at.n_mp)
        def _(dm):
            q, m = at.mate(dq, dm, 1)
            signal(sem, dp=at.z * PLANE + q, mp=m)

    @pl.loop(1, at.planes)
    def _(dz):
        _, device = at.worker(dz)
        signal(sem, **device)

    for w in range(at.per):

        @pl.when(jnp.logical_not(at.serves_own_plane(w)))
        def _():
            @pl.loop(0, at.n_mp)
            def _(m):
                signal(sem, dp=at.served(w), mp=m)

    count = (at.n_dp - 1) + (at.n_mp - 1) + (PLANE - 1) * (at.n_mp - 1) + (at.planes - 1)
    count = count + at.n_mp * at.per - jnp.where(at.is_own_worker, at.n_mp, 0)
    return lambda: pl.semaphore_wait(sem, count)


def remote(source, target, send, recv, **device):
    return pltpu.make_async_remote_copy(
        src_ref=source,
        dst_ref=target,
        send_sem=send,
        recv_sem=recv,
        device_id=device,
        device_id_type=MESH,
    )


class ToWorkers:
    def __init__(self, at, source, target, send, recv, same):
        self.at, self.source, self.target, self.send, self.recv = at, source, target, send, recv
        self.same = same

    def copy(self, dz):
        z, device = self.at.worker(dz)
        source = self.source if self.same else self.source.at[z]
        slot = (self.at.worker_slot, self.at.mp)
        return remote(source, self.target.at[slot], self.send.at[dz], self.recv.at[slot], **device)

    def start(self):
        at = self.at

        @pl.loop(1, at.planes)
        def _(dz):
            self.copy(dz).start()

        @pl.when(jnp.logical_not(at.is_own_worker))
        def _():
            self.copy(0).start()

        @pl.when(at.is_own_worker)
        def _():
            self.target[at.worker_slot, at.mp] = (
                self.source[...] if self.same else self.source[at.z]
            )

    def wait_recv(self):
        at = self.at
        for w in range(at.per):

            @pl.loop(0, at.n_mp)
            def _(m):
                @pl.when(jnp.logical_not(at.serves_own_plane(w) & (m == at.mp)))
                def _():
                    place = self.target.at[w, m]
                    remote(
                        place, place, self.send.at[0], self.recv.at[w, m], dp=at.served(w), mp=m
                    ).wait_recv()

    def wait_send(self):
        @pl.loop(1, self.at.planes)
        def _(dz):
            self.copy(dz).wait_send()

        @pl.when(jnp.logical_not(self.at.is_own_worker))
        def _():
            self.copy(0).wait_send()


class FromWorkers:
    def __init__(self, at, source, target, send, recv):
        self.at, self.source, self.target, self.send, self.recv = at, source, target, send, recv

    def copy(self, w, m):
        at = self.at
        return remote(
            self.source.at[w, m],
            self.target.at[at.z],
            self.send.at[w, m],
            self.recv.at[at.z],
            dp=at.served(w),
            mp=m,
        )

    def each(self, act):
        at = self.at
        for w in range(at.per):

            @pl.loop(0, at.n_mp)
            def _(m):
                @pl.when(jnp.logical_not(at.serves_own_plane(w) & (m == at.mp)))
                def _():
                    act(self.copy(w, m))

    def start(self):
        at = self.at
        self.each(lambda copy: copy.start())

        @pl.when(at.is_own_worker)
        def _():
            self.target[at.z] = self.source[at.worker_slot, at.mp]

    def wait_recv(self):
        at = self.at

        @pl.loop(0, at.planes)
        def _(z):
            @pl.when(jnp.logical_not(at.is_own_worker & (z == at.z)))
            def _():
                place = self.target.at[z]
                remote(
                    place,
                    place,
                    self.send.at[0, 0],
                    self.recv.at[z],
                    dp=z * PLANE + at.q,
                    mp=at.worker_mp(z),
                ).wait_recv()

    def wait_send(self):
        self.each(lambda copy: copy.wait_send())


class InPlane:
    def __init__(self, at, source, target, pick, place, send, recv):
        self.at, self.source, self.target = at, source, target
        self.pick, self.place, self.send, self.recv = pick, place, send, recv

    def copy(self, dq, dm, w):
        at = self.at
        q, m = at.mate(dq, dm, 1)
        return remote(
            self.pick(w, m, q),
            self.place(w, at.mp, at.q),
            self.send,
            self.recv,
            dp=at.z * PLANE + q,
            mp=m,
        )

    def start(self):
        def act(dq, dm):
            for w in range(self.at.per):
                self.copy(dq, dm, w).start()

        self.at.mates(act)

    def keep(self):
        at = self.at
        for w in range(at.per):
            self.place(w, at.mp, at.q)[...] = self.pick(w, at.mp, at.q)[...]

    def all(self, ref):
        ref = ref.at[pl.ds(0, self.at.per * (PLANE * self.at.n_mp - 1))]
        return remote(ref, ref, self.send, self.recv, dp=wrap(self.at.dp + 1, self.at.n_dp))

    def wait_recv(self):
        self.all(self.target).wait_recv()

    def wait_send(self):
        self.all(self.source).wait_send()


class Announce:
    def __init__(self, at, ref, send, recv):
        self.at, self.ref, self.send, self.recv = at, ref, send, recv

    def start(self):
        at = self.at
        place = self.ref.at[at.dp]

        @pl.loop(1, at.n_dp)
        def _(k):
            remote(place, place, self.send, self.recv, dp=wrap(at.dp + k, at.n_dp)).start()

    def all(self):
        ref = self.ref.at[pl.ds(0, self.at.n_dp - 1)]
        return remote(ref, ref, self.send, self.recv, dp=wrap(self.at.dp + 1, self.at.n_dp))

    def wait_recv(self):
        self.all().wait_recv()

    def wait_send(self):
        self.all().wait_send()


class Exchange:
    def __init__(self, source, target, send, recv, dp, n_dp):
        self.source, self.target, self.send, self.recv = source, target, send, recv
        self.dp, self.n_dp = dp, n_dp

    def start(self, k):
        peer = wrap(self.dp + k, self.n_dp)
        remote(
            self.source.at[peer], self.target.at[self.dp], self.send, self.recv, dp=peer
        ).start()

    def keep(self):
        self.target[pl.ds(self.dp, 1)] = self.source[pl.ds(self.dp, 1)]

    def all(self):
        pieces = pl.ds(0, self.n_dp - 1)
        return remote(
            self.source.at[pieces],
            self.target.at[pieces],
            self.send,
            self.recv,
            dp=wrap(self.dp + 1, self.n_dp),
        )

    def wait_recv(self):
        self.all().wait_recv()

    def wait_send(self):
        self.all().wait_send()


def start_all(exchanges, n_dp):
    for group in exchanges:

        @pl.loop(1, n_dp // 2)
        def _(k):
            for exchange in group:
                exchange.start(k)
                exchange.start(n_dp - k)

        for exchange in group:
            exchange.start(n_dp // 2)


class SumOverMp:
    def __init__(self, at, partial, landed, total, sems):
        self.at, self.partial, self.landed, self.total, self.sems = at, partial, landed, total, sems

    def scatter_copy(self, k):
        peer = wrap(self.at.mp + k, self.at.n_mp)
        return remote(
            self.partial.at[peer], self.landed.at[k], self.sems.at[0, k], self.sems.at[1, k], mp=peer
        )

    def spread_copy(self, k, sign):
        at = self.at
        peer = wrap(at.mp + (k if sign == 1 else at.n_mp - k), at.n_mp)
        place = self.total.at[at.mp if sign == 1 else peer]
        return remote(place, place, self.sems.at[2, k], self.sems.at[3, k], mp=peer)

    def scatter(self):
        for k in range(1, self.at.n_mp):
            self.scatter_copy(k).start()

    def summed(self):
        mine = self.partial[self.at.mp]
        for k in range(1, self.at.n_mp):
            self.scatter_copy(k).wait_recv()
            mine = mine + self.landed[k]
        return mine

    def spread(self, mine):
        self.total[self.at.mp] = mine
        for k in range(1, self.at.n_mp):
            self.spread_copy(k, 1).start()

    def arrive(self):
        for k in range(1, self.at.n_mp):
            self.spread_copy(k, -1).wait_recv()

    def wait_send(self):
        for k in range(1, self.at.n_mp):
            self.scatter_copy(k).wait_send()
            self.spread_copy(k, 1).wait_send()


def side_by_side(a):
    half = a.shape[-2] // 2
    return jnp.concatenate([a[..., :half, :], a[..., half:, :]], axis=-1)


def one_below_other(a):
    half = a.shape[-1] // 2
    return jnp.concatenate([a[..., :half], a[..., half:]], axis=-2)


def pack(a, wide):
    return jnp.concatenate([a[..., :wide], side_by_side(a[..., wide:])], axis=-2)


def unpack(a):
    rows = a.shape[-2] * 2 // 3
    return jnp.concatenate([a[..., :rows, :], one_below_other(a[..., rows:, :])], axis=-1)


def by_devices(a, columns, wide):
    return pack(a.reshape(a.shape[0] // columns, columns, a.shape[1]), wide)


def from_devices(a):
    a = unpack(a)
    return a.reshape(a.shape[0] * a.shape[1], a.shape[2])


def whole_kernel(
    n_dp,
    n_mp,
    rows_hbm,
    queries_hbm,
    keys_hbm,
    values_hbm,
    upstream_hbm,
    down_hbm,
    upq_hbm,
    upkv_hbm,
    slot_ref,
    doc_ref,
    table_ref,
    got_one,
    got_two,
    got_up_a,
    got_up_b,
    flags,
    rows_ref,
    queries_ref,
    keys_ref,
    values_ref,
    upstream_ref,
    down_ref,
    upq_ref,
    upkv_ref,
    send_panels,
    recv_panels,
    send_rows,
    recv_rows,
    send_part,
    recv_part,
    send_two,
    recv_two,
    send_up_a,
    send_up_b,
    recv_up_a,
    recv_up_b,
    partial,
    landed,
    total,
    partial_back,
    landed_back,
    total_back,
    low_one_back,
    recv_low,
    served_rows_turned,
    rows_turned,
    bias,
    grad_query_turned,
    grad_key,
    grad_value,
    send_up_a_back,
    send_up_b_back,
    send_two_back,
    send_one_back,
    load_sems,
    peer_sems,
    plane_sems,
    to_sems,
    to_sems_recv,
    from_sems,
    from_sems_recv,
    sum_sems,
):
    at = Place(n_dp, n_mp)
    dp = at.dp
    row_total, width = rows_ref.shape
    rank = down_ref.shape[2] // 3
    wide = 2 * rank
    columns = down_ref.shape[1]
    heads = queries_ref.shape[1] // LANES
    per_group = heads // 2
    group_lanes = per_group * LANES
    blocks = slot_ref.shape[0]
    block_rows = row_total // blocks
    plane_columns = width // at.planes
    inverse = 1.0 / float(LANES) ** 0.5

    loads = [
        pltpu.make_async_copy(source, target, load_sems.at[i])
        for i, (source, target) in enumerate(
            [
                (down_hbm, down_ref),
                (upq_hbm, upq_ref),
                (upkv_hbm, upkv_ref),
                (rows_hbm, rows_ref),
                (keys_hbm, keys_ref),
                (values_hbm, values_ref),
                (queries_hbm, queries_ref),
                (upstream_hbm, upstream_ref),
            ]
        )
    ]
    for load in loads:
        load.start()
    arrived = barrier(at)

    late = slot_ref[1].astype(F32)
    early = 1.0 - late
    flags[pl.ds(dp, 1)] = jnp.full((1, 1, LANES), late)
    for load in loads[:4]:
        load.wait()
    rows = rows_ref[...]
    outer_first = rows[:block_rows].astype(F32)
    outer_last = rows[row_total - block_rows :].astype(F32)
    rows_one = outer_first * late + outer_last * early
    for z in range(0, at.planes, 2):
        tile = rows_one[:, z * plane_columns : (z + 2) * plane_columns]
        send_rows[z] = side_by_side(tile[:, :plane_columns])
        send_rows[z + 1] = side_by_side(tile[:, plane_columns:])

    @pl.loop(0, n_dp, unroll=4)
    def _(d):
        first, second = table_ref[0, d], table_ref[1, d]
        a, b = down_ref[first], down_ref[second]
        send_panels[d] = jnp.concatenate(
            [a[:, :wide], b[:, :wide], jnp.concatenate([a[:, wide:], b[:, wide:]], axis=1)],
            axis=0,
        )
        a, b = upq_ref[first], upq_ref[second]
        send_up_a[d, 0] = a[:per_group]
        send_up_a[d, 1] = b[:per_group]
        send_up_a[d, 2] = jnp.concatenate([upkv_ref[first], upkv_ref[second]], axis=0)
        send_up_b[d, 0] = a[per_group:]
        send_up_b[d, 1] = b[per_group:]

    arrived()

    def exchange(index, source, target):
        return Exchange(
            source, target, peer_sems.at[2 * index], peer_sems.at[2 * index + 1], dp, n_dp
        )

    announce = Announce(at, flags, peer_sems.at[0], peer_sems.at[1])
    two_in = exchange(1, send_two, recv_two)
    up_a_in = exchange(2, send_up_a, recv_up_a)
    up_b_in = exchange(3, send_up_b, recv_up_b)
    two_back = exchange(4, send_two_back, got_two)
    up_a_back = exchange(5, send_up_a_back, got_up_a)
    up_b_back = exchange(6, send_up_b_back, got_up_b)
    rows_out = ToWorkers(at, send_rows, recv_rows, to_sems.at[0], to_sems_recv.at[0], False)
    low_out = ToWorkers(at, low_one_back, recv_low, to_sems.at[1], to_sems_recv.at[1], True)
    part_back = FromWorkers(at, send_part, recv_part, from_sems, from_sems_recv)
    panels_in = InPlane(
        at,
        send_panels,
        recv_panels,
        lambda w, m, q: send_panels.at[at.served(w, m, q)],
        lambda w, m, q: recv_panels.at[(w * n_mp + m) * PLANE + q],
        plane_sems.at[0],
        plane_sems.at[1],
    )
    one_back = InPlane(
        at,
        send_one_back,
        got_one,
        lambda w, m, q: send_one_back.at[(w * n_mp + m) * PLANE + q],
        lambda w, m, q: got_one.at[at.served(w, m, q)],
        plane_sems.at[2],
        plane_sems.at[3],
    )
    announce.start()
    rows_out.start()
    panels_in.start()
    panels_in.keep()

    rows_two = jnp.concatenate(
        [
            (outer_last * late + outer_first * early).astype(BF16),
            rows[block_rows : row_total - block_rows],
        ],
        axis=0,
    )
    announce.wait_recv()

    @pl.loop(0, n_dp, unroll=4)
    def _(d):
        second = flags[d]
        first = 1.0 - second
        panel = send_panels[d]
        narrow = panel[2 * columns :]
        narrow = narrow[:, :rank] * first[:, :rank] + narrow[:, rank:] * second[:, :rank]
        send_two[d] = jnp.concatenate(
            [
                panel[:columns] * first + panel[columns : 2 * columns] * second,
                side_by_side(narrow),
            ],
            axis=0,
        )

    start_all([[two_in]], n_dp)
    two_in.keep()
    rows_turned[...] = rows_two.T

    lane = lax.broadcasted_iota(jnp.int32, (1, row_total), 1)
    doc_lane = jnp.zeros((1, row_total), jnp.int32)
    for start in range(0, row_total, DOC_ROWS):
        doc_lane = jnp.where(lane >= start, doc_ref[start], doc_lane)
    sub = lax.broadcasted_iota(jnp.int32, (DOC_ROWS, row_total), 0)
    for start in range(0, row_total, DOC_ROWS):
        joined = (doc_lane == doc_ref[start]) & (sub + start <= lane)
        bias[start : start + DOC_ROWS] = jnp.where(joined, 0.0, MASKED).astype(F32)
    in_second = jnp.concatenate(
        [jnp.full((block_rows, LANES), slot_ref[b].astype(F32)) for b in range(blocks)], axis=0
    )
    in_first = 1.0 - in_second

    rows_out.wait_recv()
    panels_in.wait_recv()
    for w in range(at.per):
        served = jnp.concatenate(
            [one_below_other(recv_rows[w, m]) for m in range(n_mp)], axis=1
        ).astype(BF16)
        served_rows_turned[w] = served.T
        panels = jnp.concatenate(
            [
                recv_panels[
                    w * n_mp * PLANE : (w + 1) * n_mp * PLANE, i * columns : (i + 1) * columns, :
                ].reshape(n_mp * PLANE * columns, LANES)
                for i in range(3)
            ],
            axis=1,
        )
        low = dot(served, jnp.concatenate(parts(panels), axis=1), 1, 0)
        low = low[:, : 3 * LANES] + low[:, 3 * LANES :]
        first = flags[at.served(w)]
        second = 1.0 - first
        both = low[:, 2 * LANES :]
        low = jnp.concatenate(
            [
                low[:, :LANES] * first + low[:, LANES : 2 * LANES] * second,
                both[:, :rank] * first[:, :rank] + both[:, rank:] * second[:, :rank],
            ],
            axis=1,
        )
        low = pack(low, wide)
        send_part[w] = low.reshape(n_mp, low.shape[0] // n_mp, LANES)
    part_back.start()
    start_all([[up_a_in], [up_b_in]], n_dp)
    up_a_in.keep()
    up_b_in.keep()
    for load in loads[4:]:
        load.wait()

    two_in.wait_recv()
    low = dot(rows_two, jnp.concatenate(parts(from_devices(recv_two[...])), axis=1), 1, 0)
    low = pack(low[:, : 3 * rank] + low[:, 3 * rank :], wide)
    partial[...] = low.reshape(partial.shape)
    low_sum = SumOverMp(at, partial, landed, total, sum_sems.at[0])
    low_sum.scatter()
    part_back.wait_recv()
    mine_one = recv_part[0]
    for z in range(1, at.planes):
        mine_one = mine_one + recv_part[z]
    two_rows = partial.shape[1]
    one_rows = mine_one.shape[0]
    low_sum.spread(jnp.concatenate([low_sum.summed(), mine_one], axis=0))
    low_sum.arrive()
    low_two = unpack(total[:, :two_rows].reshape(n_mp * two_rows, LANES))
    low_one = unpack(total[:, two_rows:].reshape(n_mp * one_rows, LANES))
    low = jnp.concatenate(
        [
            low_one * late + low_two[:block_rows] * early,
            low_two[block_rows:],
            low_two[:block_rows] * late + low_one * early,
        ],
        axis=0,
    )

    def by_slot(low):
        return jnp.concatenate(
            [low * in_first[:, :rank], low * in_second[:, :rank]], axis=1
        )

    low_q = by_slot(low[:, :rank])
    low_k = by_slot(low[:, rank:wide])
    low_v = by_slot(low[:, wide:])

    def adapted(frozen, low, panel):
        return (frozen.astype(F32) + ADAPTER_SCALE * dot_both(low, panel, 1, 0)).astype(BF16)

    up_a_in.wait_recv()
    up_k = jnp.concatenate([recv_up_a[:, 2, 0, :], recv_up_a[:, 2, 2, :]], axis=0)
    up_v = jnp.concatenate([recv_up_a[:, 2, 1, :], recv_up_a[:, 2, 3, :]], axis=0)
    key = adapted(keys_ref[...], low_k, up_k)
    value = adapted(values_ref[...], low_v, up_v)
    key_turned = key.T
    grad_key[...] = jnp.zeros_like(grad_key)
    grad_value[...] = jnp.zeros_like(grad_value)
    grad_low_q = jnp.zeros((wide, row_total), F32)
    for g, recv_up, send_back in ((0, recv_up_a, send_up_a_back), (1, recv_up_b, send_up_b_back)):
        lanes = slice(g * group_lanes, (g + 1) * group_lanes)
        if g == 1:
            up_b_in.wait_recv()
        panel = jnp.concatenate(
            [
                jnp.concatenate([recv_up[:, 0, h, :], recv_up[:, 1, h, :]], axis=0)
                for h in range(per_group)
            ],
            axis=1,
        )
        query = adapted(queries_ref[:, lanes], low_q, panel)
        upstream = upstream_ref[:, lanes]

        def stacked(a, first):
            return jnp.concatenate(
                [
                    a[first : first + block_rows, h * LANES : (h + 1) * LANES]
                    for h in range(per_group)
                ],
                axis=0,
            )

        for b in range(blocks):
            first, last = b * block_rows, (b + 1) * block_rows
            query_b, upstream_b = stacked(query, first), stacked(upstream, first)
            mask = jnp.concatenate([bias[0:last, first:last]] * per_group, axis=1)
            scores = dot(key[:last], query_b, 1, 1) * inverse + mask
            weights = jnp.exp(scores - jnp.max(scores, axis=0, keepdims=True))
            probs = weights * (1.0 / jnp.sum(weights, axis=0, keepdims=True))
            grad_probs = dot(value[:last], upstream_b, 1, 1)
            inner = jnp.sum(probs * grad_probs, axis=0, keepdims=True)
            grad_scores = (probs * (grad_probs - inner) * inverse).astype(BF16)
            grad_key[0:last] += dot(grad_scores, query_b, 1, 0)
            grad_value[0:last] += dot(probs.astype(BF16), upstream_b, 1, 0)
            turned = dot(key_turned[:, :last], grad_scores, 1, 0)
            for h in range(per_group):
                grad_query_turned[h * LANES : (h + 1) * LANES, first:last] = turned[
                    :, h * block_rows : (h + 1) * block_rows
                ]
        grad_query = grad_query_turned[...]
        term = ADAPTER_SCALE * dot_both(grad_query, low_q, 1, 0)
        for h in range(per_group):
            turned = term[h * LANES : (h + 1) * LANES].T
            send_back[:, 0, h, :] = turned[:rank]
            send_back[:, 1, h, :] = turned[rank:]
        grad_low_q = grad_low_q + dot_both(panel, grad_query, 1, 0)
        if g == 0:
            start_all([[up_a_back]], n_dp)

    def of_slot(grad):
        return ADAPTER_SCALE * (
            grad[:, :rank] * in_first[:, :rank] + grad[:, rank:] * in_second[:, :rank]
        )

    grad_k, grad_v = grad_key[...], grad_value[...]
    grad_low = jnp.concatenate(
        [
            of_slot(grad_low_q.T),
            of_slot(dot_both(grad_k, up_k, 1, 1)),
            of_slot(dot_both(grad_v, up_v, 1, 1)),
        ],
        axis=1,
    )
    outer_first = grad_low[:block_rows]
    outer_last = grad_low[row_total - block_rows :]
    grad_one = pack(outer_first * late + outer_last * early, wide)
    grad_two = pack(
        jnp.concatenate(
            [
                outer_last * late + outer_first * early,
                grad_low[block_rows : row_total - block_rows],
            ],
            axis=0,
        ),
        wide,
    )
    partial_back[...] = jnp.concatenate(
        [grad_two.reshape(n_mp, two_rows, LANES), grad_one.reshape(n_mp, one_rows, LANES)],
        axis=1,
    )
    grad_sum = SumOverMp(at, partial_back, landed_back, total_back, sum_sems.at[1])
    term = ADAPTER_SCALE * dot_both(low_k, grad_k, 0, 0)
    send_up_b_back[:, 2, 0, :] = term[:rank]
    send_up_b_back[:, 2, 2, :] = term[rank:]
    term = ADAPTER_SCALE * dot_both(low_v, grad_v, 0, 0)
    send_up_b_back[:, 2, 1, :] = term[:rank]
    send_up_b_back[:, 2, 3, :] = term[rank:]
    grad_sum.scatter()
    start_all([[up_b_back]], n_dp)
    mine = grad_sum.summed()
    low_one_back[...] = mine[two_rows:]
    grad_sum.spread(mine[:two_rows])
    low_out.start()
    up_a_back.keep()
    up_b_back.keep()
    grad_sum.arrive()
    grads = unpack(total_back[...].reshape(n_mp * two_rows, LANES))
    term = dot(rows_turned[...], jnp.concatenate(parts(grads), axis=1), 1, 0)
    send_two_back[...] = by_devices(term[:, : 3 * rank] + term[:, 3 * rank :], columns, wide)
    start_all([[two_back]], n_dp)
    two_back.keep()

    low_out.wait_recv()
    for w in range(at.per):
        grads = unpack(recv_low[w].reshape(n_mp * one_rows, LANES))
        term = dot(served_rows_turned[w], jnp.concatenate(parts(grads), axis=1), 1, 0)
        send_one_back[w * n_mp * PLANE : (w + 1) * n_mp * PLANE] = by_devices(
            term[:, : 3 * rank] + term[:, 3 * rank :], columns, wide
        )
    one_back.start()
    one_back.keep()

    for one in (
        announce,
        rows_out,
        panels_in,
        two_in,
        part_back,
        up_a_in,
        up_b_in,
        low_sum,
        grad_sum,
        low_out,
    ):
        one.wait_send()
    for one in (up_a_back, up_b_back, one_back, two_back):
        one.wait_recv()
        one.wait_send()


def owner_kernel(
    one_ref, two_ref, up_a_ref, up_b_ref, flags_ref, table_ref, out_down, out_upq, out_upkv
):
    tenants, columns = out_down.shape[0], out_down.shape[1]
    rank = out_down.shape[2] // 3
    n_dp = one_ref.shape[0]
    per_group = up_a_ref.shape[2]
    tenant = lax.broadcasted_iota(jnp.int32, (tenants, n_dp), 0)
    owned = [
        jnp.where(tenant == table_ref[slot : slot + 1, :], 1.0, 0.0).astype(F32)
        for slot in range(2)
    ]
    late = flags_ref[:, 0, :].T[0:1, :]
    early = 1.0 - late
    owned_down = jnp.concatenate(
        [owned[0] * late + owned[1] * early, owned[1] * late + owned[0] * early], axis=1
    ).astype(BF16)
    owned_up = jnp.concatenate(owned, axis=1).astype(BF16)

    def spread(hot, count, pair, store):
        for start in range(0, count, 4):
            span = range(start, min(start + 4, count))
            terms = jnp.concatenate(
                [jnp.concatenate(pair(r), axis=0) for r in span], axis=1
            )
            total = dot_exact_left(hot, terms, 1, 0)
            for n, r in enumerate(span):
                store(r, total[:, n * LANES : (n + 1) * LANES])

    def store_down(r, total):
        if r < columns:
            out_down[:, r, 0:LANES] = total
        else:
            out_down[:, r - columns, LANES : LANES + rank] = total[:, :rank]
            out_down[:, r - columns // 2, LANES : LANES + rank] = total[:, rank:]

    spread(
        owned_down, one_ref.shape[1], lambda r: [one_ref[:, r, :], two_ref[:, r, :]], store_down
    )
    for g, ref in ((0, up_a_ref), (1, up_b_ref)):

        def store_upq(r, total, g=g):
            out_upq[:, g * per_group + r, :] = total

        spread(owned_up, per_group, lambda r, ref=ref: [ref[:, 0, r, :], ref[:, 1, r, :]], store_upq)

    def store_upkv(r, total):
        out_upkv[:, r, :] = total

    spread(owned_up, 2, lambda r: [up_b_ref[:, 2, r, :], up_b_ref[:, 2, 2 + r, :]], store_upkv)


def on_device(
    normed_input_rows,
    frozen_queries,
    frozen_keys,
    frozen_values,
    attention_output_gradient,
    adapter_down_weight,
    adapter_up_query,
    adapter_up_key_value,
    document_numbers,
    block_tenant_slot,
    shard_tenant_table,
    *,
    n_dp,
    n_mp,
):
    row_total = normed_input_rows.shape[0]
    tenants, columns, three_rank = adapter_down_weight.shape
    heads = frozen_queries.shape[1] // LANES
    upq = adapter_up_query.reshape(tenants, heads, LANES)
    upkv = adapter_up_key_value.reshape(tenants, 2, LANES)
    table = shard_tenant_table.T
    vmem = pl.BlockSpec(memory_space=pltpu.VMEM)
    smem = pl.BlockSpec(memory_space=pltpu.SMEM)
    loaded = (
        normed_input_rows,
        frozen_queries,
        frozen_keys,
        frozen_values,
        attention_output_gradient,
        adapter_down_weight,
        upq,
        upkv,
    )
    width = normed_input_rows.shape[1]
    block_rows = row_total // block_tenant_slot.shape[0]
    planes = n_dp // PLANE
    per = planes // n_mp
    one_rows = block_rows * three_rank // LANES // n_mp
    two_rows = 2 * one_rows
    all_rows = one_rows + two_rows
    piece = columns * three_rank // LANES
    send_rows_shape = (planes, block_rows * (width // planes) // LANES, LANES)

    def f32(*shape):
        return pltpu.VMEM(shape, F32)

    def dma(*shape):
        return pltpu.SemaphoreType.DMA(shape)

    outs = [
        (n_dp, piece, LANES),
        (n_dp, piece, LANES),
        (n_dp, 2, heads // 2, LANES),
        (n_dp, 3, heads // 2, LANES),
        (n_dp, 1, LANES),
    ]
    got = pl.pallas_call(
        functools.partial(whole_kernel, n_dp, n_mp),
        out_shape=[jax.ShapeDtypeStruct(s, F32) for s in outs],
        in_specs=[pl.BlockSpec(memory_space=pl.ANY)] * 8 + [smem] * 3,
        out_specs=[vmem] * len(outs),
        scratch_shapes=[
            *(pltpu.VMEM(a.shape, a.dtype) for a in loaded),
            f32(n_dp, 3 * columns, LANES),
            f32(per * n_mp * PLANE, 3 * columns, LANES),
            f32(*send_rows_shape),
            f32(per, n_mp, *send_rows_shape[1:]),
            f32(per, n_mp, one_rows, LANES),
            f32(planes, one_rows, LANES),
            f32(n_dp, piece, LANES),
            f32(n_dp, piece, LANES),
            f32(n_dp, 3, heads // 2, LANES),
            f32(n_dp, 2, heads // 2, LANES),
            f32(n_dp, 3, heads // 2, LANES),
            f32(n_dp, 2, heads // 2, LANES),
            f32(n_mp, two_rows, LANES),
            f32(n_mp, two_rows, LANES),
            f32(n_mp, all_rows, LANES),
            f32(n_mp, all_rows, LANES),
            f32(n_mp, all_rows, LANES),
            f32(n_mp, two_rows, LANES),
            f32(one_rows, LANES),
            f32(per, n_mp, one_rows, LANES),
            pltpu.VMEM((per, n_mp * PLANE * columns, block_rows), BF16),
            pltpu.VMEM((width, row_total - block_rows), BF16),
            f32(row_total, row_total),
            f32(heads // 2 * LANES, row_total),
            f32(row_total, LANES),
            f32(row_total, LANES),
            f32(n_dp, 2, heads // 2, LANES),
            f32(n_dp, 3, heads // 2, LANES),
            f32(n_dp, piece, LANES),
            f32(per * n_mp * PLANE, piece, LANES),
            dma(len(loaded)),
            dma(14),
            dma(4),
            dma(2, planes),
            dma(2, per, n_mp),
            dma(per, n_mp),
            dma(planes),
            dma(2, 4, n_mp),
        ],
        compiler_params=pltpu.CompilerParams(
            collective_id=0, has_side_effects=True, vmem_limit_bytes=60 * 1024 * 1024
        ),
        name="whole",
    )(*loaded, block_tenant_slot, document_numbers, table)
    grad_down, grad_upq, grad_upkv = pl.pallas_call(
        owner_kernel,
        out_shape=[
            jax.ShapeDtypeStruct(adapter_down_weight.shape, F32),
            jax.ShapeDtypeStruct(upq.shape, F32),
            jax.ShapeDtypeStruct(upkv.shape, F32),
        ],
        in_specs=[vmem] * 6,
        out_specs=[vmem] * 3,
        name="owner",
    )(*got, table)
    return (
        grad_down,
        grad_upq.reshape(adapter_up_query.shape),
        grad_upkv.reshape(adapter_up_key_value.shape),
    )


def solution(mesh):
    placed = (
        P("dp", "mp"),
        P("dp", "mp"),
        P("dp", "mp"),
        P("dp", "mp"),
        P("dp", "mp"),
        P(None, ("mp", "dp"), None),
        P(None, "dp", "mp"),
        P(None, "dp", "mp", None),
        P("dp"),
        P("dp"),
        P(),
    )
    return jax.shard_map(
        functools.partial(on_device, n_dp=mesh.shape["dp"], n_mp=mesh.shape["mp"]),
        mesh=mesh,
        in_specs=placed,
        out_specs=(P(None, ("mp", "dp"), None), P(None, "dp", "mp"), P(None, "dp", "mp", None)),
        check_vma=False,
    )
```

```python
import functools

import jax
import jax.numpy as jnp
from jax import lax
from jax.experimental import pallas as pl
from jax.experimental.pallas import tpu as pltpu
from jax.sharding import PartitionSpec as P

ADAPTER_SCALE = 0.5
MASKED = -1e30
MESH = pl.DeviceIdType.MESH
LANES = 128
DOC_ROWS = 16
PLANE = 4
F32 = jnp.float32
BF16 = jnp.bfloat16


def dot(a, b, ca, cb):
    return lax.dot_general(a, b, (((ca,), (cb,)), ((), ())), preferred_element_type=F32)


def parts(a):
    high = a.astype(BF16)
    return high, (a - high.astype(F32)).astype(BF16)


def dot_exact_left(a, b, ca, cb):
    high, low = parts(b)
    return dot(a, high, ca, cb) + dot(a, low, ca, cb)


def dot_both(a, b, ca, cb):
    a_high, a_low = parts(a)
    b_high, b_low = parts(b)
    return dot(a_high, b_high, ca, cb) + (dot(a_high, b_low, ca, cb) + dot(a_low, b_high, ca, cb))


def wrap(x, n):
    return jnp.where(x >= n, x - n, x)


def signal(sem, **device):
    pl.semaphore_signal(sem, inc=1, device_id=device, device_id_type=MESH)


class Place:
    def __init__(self, n_dp, n_mp):
        self.n_dp, self.n_mp = n_dp, n_mp
        self.planes = n_dp // PLANE
        self.per = self.planes // n_mp
        self.dp, self.mp = lax.axis_index("dp"), lax.axis_index("mp")
        self.z, self.q = lax.div(self.dp, PLANE), lax.rem(self.dp, PLANE)
        self.worker_slot = lax.div(self.z, n_mp)
        self.z_mp = lax.rem(self.z, n_mp)
        self.is_own_worker = self.worker_mp(self.z) == self.mp

    def worker_mp(self, z):
        return wrap(self.z_mp + wrap(z, self.n_mp), self.n_mp)

    def worker(self, dz):
        z = wrap(self.z + dz, self.planes)
        return z, {"dp": z * PLANE + self.q, "mp": self.worker_mp(z)}

    def served_z(self, w, m):
        return wrap(m + self.n_mp - self.z_mp, self.n_mp) + w * self.n_mp

    def served(self, w, m=None, q=None):
        m, q = (self.mp, self.q) if m is None else (m, q)
        return self.served_z(w, m) * PLANE + q

    def serves_own_plane(self, w):
        return self.served_z(w, self.mp) == self.z

    def mate(self, dq, dm, sign):
        if sign == 1:
            return wrap(self.q + dq, PLANE), wrap(self.mp + dm, self.n_mp)
        return wrap(self.q + PLANE - dq, PLANE), wrap(self.mp + self.n_mp - dm, self.n_mp)

    def mates(self, act):
        for dq in range(PLANE):

            @pl.loop(1 if dq == 0 else 0, self.n_mp)
            def _(dm):
                act(dq, dm)


def barrier(at):
    sem = pltpu.get_barrier_semaphore()

    @pl.loop(1, at.n_dp)
    def _(k):
        signal(sem, dp=wrap(at.dp + k, at.n_dp))

    for k in range(1, at.n_mp):
        signal(sem, mp=wrap(at.mp + k, at.n_mp))

    for dq in range(1, PLANE):

        @pl.loop(1, at.n_mp)
        def _(dm):
            q, m = at.mate(dq, dm, 1)
            signal(sem, dp=at.z * PLANE + q, mp=m)

    @pl.loop(1, at.planes)
    def _(dz):
        _, device = at.worker(dz)
        signal(sem, **device)

    for w in range(at.per):

        @pl.when(jnp.logical_not(at.serves_own_plane(w)))
        def _():
            @pl.loop(0, at.n_mp)
            def _(m):
                signal(sem, dp=at.served(w), mp=m)

    count = (at.n_dp - 1) + (at.n_mp - 1) + (PLANE - 1) * (at.n_mp - 1) + (at.planes - 1)
    count = count + at.n_mp * at.per - jnp.where(at.is_own_worker, at.n_mp, 0)
    return lambda: pl.semaphore_wait(sem, count)


def remote(source, target, send, recv, **device):
    return pltpu.make_async_remote_copy(
        src_ref=source,
        dst_ref=target,
        send_sem=send,
        recv_sem=recv,
        device_id=device,
        device_id_type=MESH,
    )


class ToWorkers:
    def __init__(self, at, source, target, send, recv, same):
        self.at, self.source, self.target, self.send, self.recv = at, source, target, send, recv
        self.same = same

    def copy(self, dz):
        z, device = self.at.worker(dz)
        source = self.source if self.same else self.source.at[z]
        slot = (self.at.worker_slot, self.at.mp)
        return remote(source, self.target.at[slot], self.send.at[dz], self.recv.at[slot], **device)

    def start(self):
        at = self.at

        @pl.loop(1, at.planes)
        def _(dz):
            self.copy(dz).start()

        @pl.when(jnp.logical_not(at.is_own_worker))
        def _():
            self.copy(0).start()

        @pl.when(at.is_own_worker)
        def _():
            self.target[at.worker_slot, at.mp] = (
                self.source[...] if self.same else self.source[at.z]
            )

    def wait_recv(self):
        at = self.at
        for w in range(at.per):

            @pl.loop(0, at.n_mp)
            def _(m):
                @pl.when(jnp.logical_not(at.serves_own_plane(w) & (m == at.mp)))
                def _():
                    place = self.target.at[w, m]
                    remote(
                        place, place, self.send.at[0], self.recv.at[w, m], dp=at.served(w), mp=m
                    ).wait_recv()

    def wait_send(self):
        @pl.loop(1, self.at.planes)
        def _(dz):
            self.copy(dz).wait_send()

        @pl.when(jnp.logical_not(self.at.is_own_worker))
        def _():
            self.copy(0).wait_send()


class FromWorkers:
    def __init__(self, at, source, target, send, recv):
        self.at, self.source, self.target, self.send, self.recv = at, source, target, send, recv

    def copy(self, w, m):
        at = self.at
        return remote(
            self.source.at[w, m],
            self.target.at[at.z],
            self.send.at[w, m],
            self.recv.at[at.z],
            dp=at.served(w),
            mp=m,
        )

    def each(self, act):
        at = self.at
        for w in range(at.per):

            @pl.loop(0, at.n_mp)
            def _(m):
                @pl.when(jnp.logical_not(at.serves_own_plane(w) & (m == at.mp)))
                def _():
                    act(self.copy(w, m))

    def start(self):
        at = self.at
        self.each(lambda copy: copy.start())

        @pl.when(at.is_own_worker)
        def _():
            self.target[at.z] = self.source[at.worker_slot, at.mp]

    def wait_recv(self):
        at = self.at

        @pl.loop(0, at.planes)
        def _(z):
            @pl.when(jnp.logical_not(at.is_own_worker & (z == at.z)))
            def _():
                place = self.target.at[z]
                remote(
                    place,
                    place,
                    self.send.at[0, 0],
                    self.recv.at[z],
                    dp=z * PLANE + at.q,
                    mp=at.worker_mp(z),
                ).wait_recv()

    def wait_send(self):
        self.each(lambda copy: copy.wait_send())


class InPlane:
    def __init__(self, at, source, target, pick, place, send, recv):
        self.at, self.source, self.target = at, source, target
        self.pick, self.place, self.send, self.recv = pick, place, send, recv

    def copy(self, dq, dm, w):
        at = self.at
        q, m = at.mate(dq, dm, 1)
        return remote(
            self.pick(w, m, q),
            self.place(w, at.mp, at.q),
            self.send,
            self.recv,
            dp=at.z * PLANE + q,
            mp=m,
        )

    def start(self):
        def act(dq, dm):
            for w in range(self.at.per):
                self.copy(dq, dm, w).start()

        self.at.mates(act)

    def keep(self):
        at = self.at
        for w in range(at.per):
            self.place(w, at.mp, at.q)[...] = self.pick(w, at.mp, at.q)[...]

    def all(self, ref):
        ref = ref.at[pl.ds(0, self.at.per * (PLANE * self.at.n_mp - 1))]
        return remote(ref, ref, self.send, self.recv, dp=wrap(self.at.dp + 1, self.at.n_dp))

    def wait_recv(self):
        self.all(self.target).wait_recv()

    def wait_send(self):
        self.all(self.source).wait_send()


class Announce:
    def __init__(self, at, ref, send, recv):
        self.at, self.ref, self.send, self.recv = at, ref, send, recv

    def start(self):
        at = self.at
        place = self.ref.at[at.dp]

        @pl.loop(1, at.n_dp)
        def _(k):
            remote(place, place, self.send, self.recv, dp=wrap(at.dp + k, at.n_dp)).start()

    def all(self):
        ref = self.ref.at[pl.ds(0, self.at.n_dp - 1)]
        return remote(ref, ref, self.send, self.recv, dp=wrap(self.at.dp + 1, self.at.n_dp))

    def wait_recv(self):
        self.all().wait_recv()

    def wait_send(self):
        self.all().wait_send()


class Exchange:
    def __init__(self, source, target, send, recv, dp, n_dp):
        self.source, self.target, self.send, self.recv = source, target, send, recv
        self.dp, self.n_dp = dp, n_dp

    def start(self, k):
        peer = wrap(self.dp + k, self.n_dp)
        remote(
            self.source.at[peer], self.target.at[self.dp], self.send, self.recv, dp=peer
        ).start()

    def keep(self):
        self.target[pl.ds(self.dp, 1)] = self.source[pl.ds(self.dp, 1)]

    def all(self):
        pieces = pl.ds(0, self.n_dp - 1)
        return remote(
            self.source.at[pieces],
            self.target.at[pieces],
            self.send,
            self.recv,
            dp=wrap(self.dp + 1, self.n_dp),
        )

    def wait_recv(self):
        self.all().wait_recv()

    def wait_send(self):
        self.all().wait_send()


def start_all(exchanges, n_dp):
    for group in exchanges:

        @pl.loop(1, n_dp // 2)
        def _(k):
            for exchange in group:
                exchange.start(k)
                exchange.start(n_dp - k)

        for exchange in group:
            exchange.start(n_dp // 2)


class SumOverMp:
    def __init__(self, at, partial, landed, total, sems):
        self.at, self.partial, self.landed, self.total, self.sems = at, partial, landed, total, sems

    def scatter_copy(self, k):
        peer = wrap(self.at.mp + k, self.at.n_mp)
        return remote(
            self.partial.at[peer], self.landed.at[k], self.sems.at[0, k], self.sems.at[1, k], mp=peer
        )

    def spread_copy(self, k, sign):
        at = self.at
        peer = wrap(at.mp + (k if sign == 1 else at.n_mp - k), at.n_mp)
        place = self.total.at[at.mp if sign == 1 else peer]
        return remote(place, place, self.sems.at[2, k], self.sems.at[3, k], mp=peer)

    def scatter(self):
        for k in range(1, self.at.n_mp):
            self.scatter_copy(k).start()

    def summed(self):
        mine = self.partial[self.at.mp]
        for k in range(1, self.at.n_mp):
            self.scatter_copy(k).wait_recv()
            mine = mine + self.landed[k]
        return mine

    def spread(self, mine):
        self.total[self.at.mp] = mine
        for k in range(1, self.at.n_mp):
            self.spread_copy(k, 1).start()

    def arrive(self):
        for k in range(1, self.at.n_mp):
            self.spread_copy(k, -1).wait_recv()

    def wait_send(self):
        for k in range(1, self.at.n_mp):
            self.scatter_copy(k).wait_send()
            self.spread_copy(k, 1).wait_send()


def side_by_side(a):
    half = a.shape[-2] // 2
    return jnp.concatenate([a[..., :half, :], a[..., half:, :]], axis=-1)


def one_below_other(a):
    half = a.shape[-1] // 2
    return jnp.concatenate([a[..., :half], a[..., half:]], axis=-2)


def pack(a, wide):
    return jnp.concatenate([a[..., :wide], side_by_side(a[..., wide:])], axis=-2)


def unpack(a):
    rows = a.shape[-2] * 2 // 3
    return jnp.concatenate([a[..., :rows, :], one_below_other(a[..., rows:, :])], axis=-1)


def by_devices(a, columns, wide):
    return pack(a.reshape(a.shape[0] // columns, columns, a.shape[1]), wide)


def from_devices(a):
    a = unpack(a)
    return a.reshape(a.shape[0] * a.shape[1], a.shape[2])


def whole_kernel(
    n_dp,
    n_mp,
    rows_hbm,
    queries_hbm,
    keys_hbm,
    values_hbm,
    upstream_hbm,
    down_hbm,
    upq_hbm,
    upkv_hbm,
    slot_ref,
    doc_ref,
    table_ref,
    got_one,
    got_two,
    got_up_a,
    got_up_b,
    flags,
    rows_ref,
    queries_ref,
    keys_ref,
    values_ref,
    upstream_ref,
    down_ref,
    upq_ref,
    upkv_ref,
    send_panels,
    recv_panels,
    send_rows,
    recv_rows,
    send_part,
    recv_part,
    send_two,
    recv_two,
    send_up_a,
    send_up_b,
    recv_up_a,
    recv_up_b,
    partial,
    landed,
    total,
    partial_back,
    landed_back,
    total_back,
    low_one_back,
    recv_low,
    served_rows_turned,
    rows_turned,
    bias,
    grad_query_turned,
    grad_key,
    grad_value,
    send_up_a_back,
    send_up_b_back,
    send_two_back,
    send_one_back,
    load_sems,
    peer_sems,
    plane_sems,
    to_sems,
    to_sems_recv,
    from_sems,
    from_sems_recv,
    sum_sems,
):
    at = Place(n_dp, n_mp)
    dp = at.dp
    row_total, width = rows_ref.shape
    rank = down_ref.shape[2] // 3
    wide = 2 * rank
    columns = down_ref.shape[1]
    heads = queries_ref.shape[1] // LANES
    per_group = heads // 2
    group_lanes = per_group * LANES
    blocks = slot_ref.shape[0]
    block_rows = row_total // blocks
    plane_columns = width // at.planes
    inverse = 1.0 / float(LANES) ** 0.5

    loads = [
        pltpu.make_async_copy(source, target, load_sems.at[i])
        for i, (source, target) in enumerate(
            [
                (down_hbm, down_ref),
                (upq_hbm, upq_ref),
                (upkv_hbm, upkv_ref),
                (rows_hbm, rows_ref),
                (keys_hbm, keys_ref),
                (values_hbm, values_ref),
                (queries_hbm, queries_ref),
                (upstream_hbm, upstream_ref),
            ]
        )
    ]
    for load in loads:
        load.start()
    arrived = barrier(at)

    late = slot_ref[1].astype(F32)
    early = 1.0 - late
    flags[pl.ds(dp, 1)] = jnp.full((1, 1, LANES), late)
    for load in loads[:4]:
        load.wait()
    rows = rows_ref[...]
    outer_first = rows[:block_rows].astype(F32)
    outer_last = rows[row_total - block_rows :].astype(F32)
    rows_one = outer_first * late + outer_last * early
    for z in range(0, at.planes, 2):
        tile = rows_one[:, z * plane_columns : (z + 2) * plane_columns]
        send_rows[z] = side_by_side(tile[:, :plane_columns])
        send_rows[z + 1] = side_by_side(tile[:, plane_columns:])

    @pl.loop(0, n_dp, unroll=4)
    def _(d):
        first, second = table_ref[0, d], table_ref[1, d]
        a, b = down_ref[first], down_ref[second]
        send_panels[d] = jnp.concatenate(
            [a[:, :wide], b[:, :wide], jnp.concatenate([a[:, wide:], b[:, wide:]], axis=1)],
            axis=0,
        )
        a, b = upq_ref[first], upq_ref[second]
        send_up_a[d, 0] = a[:per_group]
        send_up_a[d, 1] = b[:per_group]
        send_up_a[d, 2] = jnp.concatenate([upkv_ref[first], upkv_ref[second]], axis=0)
        send_up_b[d, 0] = a[per_group:]
        send_up_b[d, 1] = b[per_group:]

    arrived()

    def exchange(index, source, target):
        return Exchange(
            source, target, peer_sems.at[2 * index], peer_sems.at[2 * index + 1], dp, n_dp
        )

    announce = Announce(at, flags, peer_sems.at[0], peer_sems.at[1])
    two_in = exchange(1, send_two, recv_two)
    up_a_in = exchange(2, send_up_a, recv_up_a)
    up_b_in = exchange(3, send_up_b, recv_up_b)
    two_back = exchange(4, send_two_back, got_two)
    up_a_back = exchange(5, send_up_a_back, got_up_a)
    up_b_back = exchange(6, send_up_b_back, got_up_b)
    rows_out = ToWorkers(at, send_rows, recv_rows, to_sems.at[0], to_sems_recv.at[0], False)
    low_out = ToWorkers(at, low_one_back, recv_low, to_sems.at[1], to_sems_recv.at[1], True)
    part_back = FromWorkers(at, send_part, recv_part, from_sems, from_sems_recv)
    panels_in = InPlane(
        at,
        send_panels,
        recv_panels,
        lambda w, m, q: send_panels.at[at.served(w, m, q)],
        lambda w, m, q: recv_panels.at[(w * n_mp + m) * PLANE + q],
        plane_sems.at[0],
        plane_sems.at[1],
    )
    one_back = InPlane(
        at,
        send_one_back,
        got_one,
        lambda w, m, q: send_one_back.at[(w * n_mp + m) * PLANE + q],
        lambda w, m, q: got_one.at[at.served(w, m, q)],
        plane_sems.at[2],
        plane_sems.at[3],
    )
    announce.start()
    rows_out.start()
    panels_in.start()
    panels_in.keep()

    rows_two = jnp.concatenate(
        [
            (outer_last * late + outer_first * early).astype(BF16),
            rows[block_rows : row_total - block_rows],
        ],
        axis=0,
    )
    announce.wait_recv()

    @pl.loop(0, n_dp, unroll=4)
    def _(d):
        second = flags[d]
        first = 1.0 - second
        panel = send_panels[d]
        narrow = panel[2 * columns :]
        narrow = narrow[:, :rank] * first[:, :rank] + narrow[:, rank:] * second[:, :rank]
        send_two[d] = jnp.concatenate(
            [
                panel[:columns] * first + panel[columns : 2 * columns] * second,
                side_by_side(narrow),
            ],
            axis=0,
        )

    start_all([[two_in]], n_dp)
    two_in.keep()
    rows_turned[...] = rows_two.T

    lane = lax.broadcasted_iota(jnp.int32, (1, row_total), 1)
    doc_lane = jnp.zeros((1, row_total), jnp.int32)
    for start in range(0, row_total, DOC_ROWS):
        doc_lane = jnp.where(lane >= start, doc_ref[start], doc_lane)
    sub = lax.broadcasted_iota(jnp.int32, (DOC_ROWS, row_total), 0)
    for start in range(0, row_total, DOC_ROWS):
        joined = (doc_lane == doc_ref[start]) & (sub + start <= lane)
        bias[start : start + DOC_ROWS] = jnp.where(joined, 0.0, MASKED).astype(F32)
    in_second = jnp.concatenate(
        [jnp.full((block_rows, LANES), slot_ref[b].astype(F32)) for b in range(blocks)], axis=0
    )
    in_first = 1.0 - in_second

    rows_out.wait_recv()
    panels_in.wait_recv()
    for w in range(at.per):
        served = jnp.concatenate(
            [one_below_other(recv_rows[w, m]) for m in range(n_mp)], axis=1
        ).astype(BF16)
        served_rows_turned[w] = served.T
        panels = jnp.concatenate(
            [
                recv_panels[
                    w * n_mp * PLANE : (w + 1) * n_mp * PLANE, i * columns : (i + 1) * columns, :
                ].reshape(n_mp * PLANE * columns, LANES)
                for i in range(3)
            ],
            axis=1,
        )
        low = dot(served, jnp.concatenate(parts(panels), axis=1), 1, 0)
        low = low[:, : 3 * LANES] + low[:, 3 * LANES :]
        first = flags[at.served(w)]
        second = 1.0 - first
        both = low[:, 2 * LANES :]
        low = jnp.concatenate(
            [
                low[:, :LANES] * first + low[:, LANES : 2 * LANES] * second,
                both[:, :rank] * first[:, :rank] + both[:, rank:] * second[:, :rank],
            ],
            axis=1,
        )
        low = pack(low, wide)
        send_part[w] = low.reshape(n_mp, low.shape[0] // n_mp, LANES)
    part_back.start()
    start_all([[up_a_in], [up_b_in]], n_dp)
    up_a_in.keep()
    up_b_in.keep()
    for load in loads[4:]:
        load.wait()

    two_in.wait_recv()
    low = dot(rows_two, jnp.concatenate(parts(from_devices(recv_two[...])), axis=1), 1, 0)
    low = pack(low[:, : 3 * rank] + low[:, 3 * rank :], wide)
    partial[...] = low.reshape(partial.shape)
    low_sum = SumOverMp(at, partial, landed, total, sum_sems.at[0])
    low_sum.scatter()
    part_back.wait_recv()
    mine_one = recv_part[0]
    for z in range(1, at.planes):
        mine_one = mine_one + recv_part[z]
    two_rows = partial.shape[1]
    one_rows = mine_one.shape[0]
    low_sum.spread(jnp.concatenate([low_sum.summed(), mine_one], axis=0))
    low_sum.arrive()
    low_two = unpack(total[:, :two_rows].reshape(n_mp * two_rows, LANES))
    low_one = unpack(total[:, two_rows:].reshape(n_mp * one_rows, LANES))
    low = jnp.concatenate(
        [
            low_one * late + low_two[:block_rows] * early,
            low_two[block_rows:],
            low_two[:block_rows] * late + low_one * early,
        ],
        axis=0,
    )

    def by_slot(low):
        return jnp.concatenate(
            [low * in_first[:, :rank], low * in_second[:, :rank]], axis=1
        )

    low_q = by_slot(low[:, :rank])
    low_k = by_slot(low[:, rank:wide])
    low_v = by_slot(low[:, wide:])

    def adapted(frozen, low, panel):
        return (frozen.astype(F32) + ADAPTER_SCALE * dot_both(low, panel, 1, 0)).astype(BF16)

    up_a_in.wait_recv()
    up_k = jnp.concatenate([recv_up_a[:, 2, 0, :], recv_up_a[:, 2, 2, :]], axis=0)
    up_v = jnp.concatenate([recv_up_a[:, 2, 1, :], recv_up_a[:, 2, 3, :]], axis=0)
    key = adapted(keys_ref[...], low_k, up_k)
    value = adapted(values_ref[...], low_v, up_v)
    key_turned = key.T
    grad_key[...] = jnp.zeros_like(grad_key)
    grad_value[...] = jnp.zeros_like(grad_value)
    grad_low_q = jnp.zeros((wide, row_total), F32)
    for g, recv_up, send_back in ((0, recv_up_a, send_up_a_back), (1, recv_up_b, send_up_b_back)):
        lanes = slice(g * group_lanes, (g + 1) * group_lanes)
        if g == 1:
            up_b_in.wait_recv()
        panel = jnp.concatenate(
            [
                jnp.concatenate([recv_up[:, 0, h, :], recv_up[:, 1, h, :]], axis=0)
                for h in range(per_group)
            ],
            axis=1,
        )
        query = adapted(queries_ref[:, lanes], low_q, panel)
        upstream = upstream_ref[:, lanes]

        def stacked(a, first):
            return jnp.concatenate(
                [
                    a[first : first + block_rows, h * LANES : (h + 1) * LANES]
                    for h in range(per_group)
                ],
                axis=0,
            )

        for b in range(blocks):
            first, last = b * block_rows, (b + 1) * block_rows
            query_b, upstream_b = stacked(query, first), stacked(upstream, first)
            mask = jnp.concatenate([bias[0:last, first:last]] * per_group, axis=1)
            scores = dot(key[:last], query_b, 1, 1) * inverse + mask
            weights = jnp.exp(scores - jnp.max(scores, axis=0, keepdims=True))
            probs = weights * (1.0 / jnp.sum(weights, axis=0, keepdims=True))
            grad_probs = dot(value[:last], upstream_b, 1, 1)
            inner = jnp.sum(probs * grad_probs, axis=0, keepdims=True)
            grad_scores = (probs * (grad_probs - inner) * inverse).astype(BF16)
            grad_key[0:last] += dot(grad_scores, query_b, 1, 0)
            grad_value[0:last] += dot(probs.astype(BF16), upstream_b, 1, 0)
            turned = dot(key_turned[:, :last], grad_scores, 1, 0)
            for h in range(per_group):
                grad_query_turned[h * LANES : (h + 1) * LANES, first:last] = turned[
                    :, h * block_rows : (h + 1) * block_rows
                ]
        grad_query = grad_query_turned[...]
        term = ADAPTER_SCALE * dot_both(grad_query, low_q, 1, 0)
        for h in range(per_group):
            turned = term[h * LANES : (h + 1) * LANES].T
            send_back[:, 0, h, :] = turned[:rank]
            send_back[:, 1, h, :] = turned[rank:]
        grad_low_q = grad_low_q + dot_both(panel, grad_query, 1, 0)
        if g == 0:
            start_all([[up_a_back]], n_dp)

    def of_slot(grad):
        return ADAPTER_SCALE * (
            grad[:, :rank] * in_first[:, :rank] + grad[:, rank:] * in_second[:, :rank]
        )

    grad_k, grad_v = grad_key[...], grad_value[...]
    grad_low = jnp.concatenate(
        [
            of_slot(grad_low_q.T),
            of_slot(dot_both(grad_k, up_k, 1, 1)),
            of_slot(dot_both(grad_v, up_v, 1, 1)),
        ],
        axis=1,
    )
    outer_first = grad_low[:block_rows]
    outer_last = grad_low[row_total - block_rows :]
    grad_one = pack(outer_first * late + outer_last * early, wide)
    grad_two = pack(
        jnp.concatenate(
            [
                outer_last * late + outer_first * early,
                grad_low[block_rows : row_total - block_rows],
            ],
            axis=0,
        ),
        wide,
    )
    partial_back[...] = jnp.concatenate(
        [grad_two.reshape(n_mp, two_rows, LANES), grad_one.reshape(n_mp, one_rows, LANES)],
        axis=1,
    )
    grad_sum = SumOverMp(at, partial_back, landed_back, total_back, sum_sems.at[1])
    term = ADAPTER_SCALE * dot_both(low_k, grad_k, 0, 0)
    send_up_b_back[:, 2, 0, :] = term[:rank]
    send_up_b_back[:, 2, 2, :] = term[rank:]
    term = ADAPTER_SCALE * dot_both(low_v, grad_v, 0, 0)
    send_up_b_back[:, 2, 1, :] = term[:rank]
    send_up_b_back[:, 2, 3, :] = term[rank:]
    grad_sum.scatter()
    start_all([[up_b_back]], n_dp)
    mine = grad_sum.summed()
    low_one_back[...] = mine[two_rows:]
    grad_sum.spread(mine[:two_rows])
    low_out.start()
    up_a_back.keep()
    up_b_back.keep()
    grad_sum.arrive()
    grads = unpack(total_back[...].reshape(n_mp * two_rows, LANES))
    term = dot(rows_turned[...], jnp.concatenate(parts(grads), axis=1), 1, 0)
    send_two_back[...] = by_devices(term[:, : 3 * rank] + term[:, 3 * rank :], columns, wide)
    start_all([[two_back]], n_dp)
    two_back.keep()

    low_out.wait_recv()
    for w in range(at.per):
        grads = unpack(recv_low[w].reshape(n_mp * one_rows, LANES))
        term = dot(served_rows_turned[w], jnp.concatenate(parts(grads), axis=1), 1, 0)
        send_one_back[w * n_mp * PLANE : (w + 1) * n_mp * PLANE] = by_devices(
            term[:, : 3 * rank] + term[:, 3 * rank :], columns, wide
        )
    one_back.start()
    one_back.keep()

    for one in (
        announce,
        rows_out,
        panels_in,
        two_in,
        part_back,
        up_a_in,
        up_b_in,
        low_sum,
        grad_sum,
        low_out,
    ):
        one.wait_send()
    for one in (up_a_back, up_b_back, one_back, two_back):
        one.wait_recv()
        one.wait_send()


def owner_kernel(
    one_hbm,
    two_hbm,
    up_a_hbm,
    up_b_hbm,
    flags_ref,
    table_ref,
    down_hbm,
    upq_hbm,
    upkv_hbm,
    one_ref,
    two_ref,
    up_a_ref,
    up_b_ref,
    out_down,
    out_upq,
    out_upkv,
    sems,
):
    pairs = [
        (up_a_hbm, up_a_ref),
        (up_b_hbm, up_b_ref),
        (one_hbm, one_ref),
        (two_hbm, two_ref),
        (out_upq, upq_hbm),
        (out_upkv, upkv_hbm),
        (out_down, down_hbm),
    ]
    copies = [pltpu.make_async_copy(a, b, sems.at[i]) for i, (a, b) in enumerate(pairs)]
    for copy in copies[:4]:
        copy.start()
    tenants, columns = out_down.shape[0], out_down.shape[1]
    rank = out_down.shape[2] // 3
    n_dp = one_ref.shape[0]
    per_group = up_a_ref.shape[2]
    tenant = lax.broadcasted_iota(jnp.int32, (tenants, n_dp), 0)
    owned = [
        jnp.where(tenant == table_ref[slot : slot + 1, :], 1.0, 0.0).astype(F32)
        for slot in range(2)
    ]
    late = flags_ref[:, 0, :].T[0:1, :]
    early = 1.0 - late
    owned_down = jnp.concatenate(
        [owned[0] * late + owned[1] * early, owned[1] * late + owned[0] * early], axis=1
    ).astype(BF16)
    owned_up = jnp.concatenate(owned, axis=1).astype(BF16)

    def spread(hot, count, pair, store):
        for start in range(0, count, 4):
            span = range(start, min(start + 4, count))
            terms = jnp.concatenate(
                [jnp.concatenate(pair(r), axis=0) for r in span], axis=1
            )
            total = dot_exact_left(hot, terms, 1, 0)
            for n, r in enumerate(span):
                store(r, total[:, n * LANES : (n + 1) * LANES])

    def store_down(r, total):
        if r < columns:
            out_down[:, r, 0:LANES] = total
        else:
            out_down[:, r - columns, LANES : LANES + rank] = total[:, :rank]
            out_down[:, r - columns // 2, LANES : LANES + rank] = total[:, rank:]

    for copy in copies[:2]:
        copy.wait()
    for g, ref in ((0, up_a_ref), (1, up_b_ref)):

        def store_upq(r, total, g=g):
            out_upq[:, g * per_group + r, :] = total

        spread(owned_up, per_group, lambda r, ref=ref: [ref[:, 0, r, :], ref[:, 1, r, :]], store_upq)

    def store_upkv(r, total):
        out_upkv[:, r, :] = total

    spread(owned_up, 2, lambda r: [up_b_ref[:, 2, r, :], up_b_ref[:, 2, 2 + r, :]], store_upkv)
    for copy in copies[4:6]:
        copy.start()
    for copy in copies[2:4]:
        copy.wait()
    spread(
        owned_down, one_ref.shape[1], lambda r: [one_ref[:, r, :], two_ref[:, r, :]], store_down
    )
    copies[6].start()
    for copy in copies[4:]:
        copy.wait()


def on_device(
    normed_input_rows,
    frozen_queries,
    frozen_keys,
    frozen_values,
    attention_output_gradient,
    adapter_down_weight,
    adapter_up_query,
    adapter_up_key_value,
    document_numbers,
    block_tenant_slot,
    shard_tenant_table,
    *,
    n_dp,
    n_mp,
):
    row_total = normed_input_rows.shape[0]
    tenants, columns, three_rank = adapter_down_weight.shape
    heads = frozen_queries.shape[1] // LANES
    upq = adapter_up_query.reshape(tenants, heads, LANES)
    upkv = adapter_up_key_value.reshape(tenants, 2, LANES)
    table = shard_tenant_table.T
    vmem = pl.BlockSpec(memory_space=pltpu.VMEM)
    smem = pl.BlockSpec(memory_space=pltpu.SMEM)
    loaded = (
        normed_input_rows,
        frozen_queries,
        frozen_keys,
        frozen_values,
        attention_output_gradient,
        adapter_down_weight,
        upq,
        upkv,
    )
    width = normed_input_rows.shape[1]
    block_rows = row_total // block_tenant_slot.shape[0]
    planes = n_dp // PLANE
    per = planes // n_mp
    one_rows = block_rows * three_rank // LANES // n_mp
    two_rows = 2 * one_rows
    all_rows = one_rows + two_rows
    piece = columns * three_rank // LANES
    send_rows_shape = (planes, block_rows * (width // planes) // LANES, LANES)

    def f32(*shape):
        return pltpu.VMEM(shape, F32)

    def dma(*shape):
        return pltpu.SemaphoreType.DMA(shape)

    outs = [
        (n_dp, piece, LANES),
        (n_dp, piece, LANES),
        (n_dp, 2, heads // 2, LANES),
        (n_dp, 3, heads // 2, LANES),
        (n_dp, 1, LANES),
    ]
    got = pl.pallas_call(
        functools.partial(whole_kernel, n_dp, n_mp),
        out_shape=[jax.ShapeDtypeStruct(s, F32) for s in outs],
        in_specs=[pl.BlockSpec(memory_space=pl.ANY)] * 8 + [smem] * 3,
        out_specs=[vmem] * len(outs),
        scratch_shapes=[
            *(pltpu.VMEM(a.shape, a.dtype) for a in loaded),
            f32(n_dp, 3 * columns, LANES),
            f32(per * n_mp * PLANE, 3 * columns, LANES),
            f32(*send_rows_shape),
            f32(per, n_mp, *send_rows_shape[1:]),
            f32(per, n_mp, one_rows, LANES),
            f32(planes, one_rows, LANES),
            f32(n_dp, piece, LANES),
            f32(n_dp, piece, LANES),
            f32(n_dp, 3, heads // 2, LANES),
            f32(n_dp, 2, heads // 2, LANES),
            f32(n_dp, 3, heads // 2, LANES),
            f32(n_dp, 2, heads // 2, LANES),
            f32(n_mp, two_rows, LANES),
            f32(n_mp, two_rows, LANES),
            f32(n_mp, all_rows, LANES),
            f32(n_mp, all_rows, LANES),
            f32(n_mp, all_rows, LANES),
            f32(n_mp, two_rows, LANES),
            f32(one_rows, LANES),
            f32(per, n_mp, one_rows, LANES),
            pltpu.VMEM((per, n_mp * PLANE * columns, block_rows), BF16),
            pltpu.VMEM((width, row_total - block_rows), BF16),
            f32(row_total, row_total),
            f32(heads // 2 * LANES, row_total),
            f32(row_total, LANES),
            f32(row_total, LANES),
            f32(n_dp, 2, heads // 2, LANES),
            f32(n_dp, 3, heads // 2, LANES),
            f32(n_dp, piece, LANES),
            f32(per * n_mp * PLANE, piece, LANES),
            dma(len(loaded)),
            dma(14),
            dma(4),
            dma(2, planes),
            dma(2, per, n_mp),
            dma(per, n_mp),
            dma(planes),
            dma(2, 4, n_mp),
        ],
        compiler_params=pltpu.CompilerParams(
            collective_id=0, has_side_effects=True, vmem_limit_bytes=60 * 1024 * 1024
        ),
        name="whole",
    )(*loaded, block_tenant_slot, document_numbers, table)
    grad_down, grad_upq, grad_upkv = pl.pallas_call(
        owner_kernel,
        out_shape=[
            jax.ShapeDtypeStruct(adapter_down_weight.shape, F32),
            jax.ShapeDtypeStruct(upq.shape, F32),
            jax.ShapeDtypeStruct(upkv.shape, F32),
        ],
        in_specs=[pl.BlockSpec(memory_space=pl.ANY)] * 4 + [vmem] * 2,
        out_specs=[pl.BlockSpec(memory_space=pl.ANY)] * 3,
        scratch_shapes=[
            *(f32(*shape) for shape in outs[:4]),
            f32(*adapter_down_weight.shape),
            f32(*upq.shape),
            f32(*upkv.shape),
            dma(7),
        ],
        name="owner",
    )(*got, table)
    return (
        grad_down,
        grad_upq.reshape(adapter_up_query.shape),
        grad_upkv.reshape(adapter_up_key_value.shape),
    )


def solution(mesh):
    placed = (
        P("dp", "mp"),
        P("dp", "mp"),
        P("dp", "mp"),
        P("dp", "mp"),
        P("dp", "mp"),
        P(None, ("mp", "dp"), None),
        P(None, "dp", "mp"),
        P(None, "dp", "mp", None),
        P("dp"),
        P("dp"),
        P(),
    )
    return jax.shard_map(
        functools.partial(on_device, n_dp=mesh.shape["dp"], n_mp=mesh.shape["mp"]),
        mesh=mesh,
        in_specs=placed,
        out_specs=(P(None, ("mp", "dp"), None), P(None, "dp", "mp"), P(None, "dp", "mp", None)),
        check_vma=False,
    )
```
